32 devices in a mesh: groups: 2 (over y), box: 4 (over z), sub: 2 (over x), rep: 2 (over core).
Axes of the slice: x: 2, y: 2, z: 4, core: 2. Of those that a mesh axis runs over, the one named last changes fastest.
Arguments:
- atom_data: float32 [16, 24, 4, 128], P(('groups', 'box', 'rep')), parts along dimension 0, may hold values from -0.8 to 64, as said below
- atom_type: int32 [16, 24, 128], P(('groups', 'box', 'rep')), parts along dimension 0, may hold values from 0 to 31
- tile_info: int32 [16, 24, 2], P(('groups', 'box', 'rep')), parts along dimension 0, may hold values from 1 to 128, as said below
- lj_repulsion: float32 [32], replicated, may hold values from 100 to 1000
- lj_dispersion: float32 [32], replicated, may hold values from 3 to 30
- send_tiles: int32 [16, 2, 8, 3], P(('groups', 'box', 'rep'), 'sub'), parts along dimension 0, may hold values from 0 to 23, as said below
- send_count: int32 [16, 2, 8], P(('groups', 'box', 'rep'), 'sub'), parts along dimension 0, may hold values from 1 to 3
- pair_slots: int32 [16, 2, 192, 2], P(('groups', 'box', 'rep'), 'sub'), parts along dimension 0, may hold values from 0 to 23, as said below
- pair_count: int32 [16, 2], P(('groups', 'box', 'rep'), 'sub'), parts along dimension 0, may hold values from 1 to 192
Outputs:
- forces: float32 [16, 24, 3, 128], P(('groups', 'box', 'rep'), 'sub'), parts along dimension 0
The draws below stay inside these ranges and needn't reach their ends.
There are 2 independent parts, one for each index of `groups`. The reference program is written for one: setup_inputs(seed, part) draws one part's arguments, and reference() takes and returns one part's arrays. A program takes and returns all parts, laid end to end along the dimension named above; an argument that names none is the same for every part. Nothing has to cross between parts.
Inputs may be any that keep to these rules, and one draw needn't show every extreme that they name: `tile_info`: column 0 lies in 64 to 128, column 1 in 1 to 4. `send_tiles`: the 3 entries of a row are distinct. `pair_slots`: each slot w * 3 + c has c < send_count[w, s, h] for the device (h, s) that holds the pair. `atom_data`: rows 0 to 2 are coordinates in angstrom, row 3 the charge.
All inputs are finite; a program needn't handle non-finite values.
Results may differ from the reference program's by a relative error of at most 0.0003.
Values sent between devices are 32-bit elements; how exact they have to be, the bound alone decides.
A program may use at most 64 MiB of HBM per device.

```python
import math
import jax
import jax.numpy as jnp
from jax import lax

TILE = 128
HT = 24
CAP = 3
PAIRS_DEV = 192
NTYPE = 32
HOMES = 8
N_SUB = 2
N_REP = 2


def send_counts_of(key):
    counts = jax.random.randint(jax.random.fold_in(key, 101), (HOMES, N_SUB, HOMES), 1, CAP + 1)
    column = jax.random.randint(jax.random.fold_in(key, 102), (N_SUB,), 0, HOMES)
    shifted = jax.random.randint(jax.random.fold_in(key, 103), (), 0, HOMES)
    home_ids = jnp.arange(HOMES)
    full_column = home_ids[None, None, :] == column[None, :, None]
    diagonal = home_ids[None, None, :] == ((home_ids + shifted) % HOMES)[:, None, None]
    return jnp.where(full_column | diagonal, CAP, counts).astype(jnp.int32)


def draw_send_count(key, part):
    return send_counts_of(key)


def draw_send_tiles(key, part):
    scores = jax.random.randint(jax.random.fold_in(key, 104), (HOMES, N_SUB, HOMES, HT), 0, 1 << 20)
    scores = scores * HT + jnp.arange(HT)
    return jnp.argsort(scores, axis=-1)[..., :CAP].astype(jnp.int32)


def draw_pair_slots(key, part):
    counts = send_counts_of(key)
    shape = (HOMES, N_SUB, PAIRS_DEV)
    receiver = jnp.arange(HOMES)[:, None, None]
    plane_ids = jnp.arange(N_SUB)[None, :, None]
    near_home = jax.random.randint(jax.random.fold_in(key, 105), shape, 0, HOMES)
    near_col = jax.random.randint(jax.random.fold_in(key, 106), shape, 0, 1 << 16) % counts[near_home, plane_ids, receiver]
    box_total = HOMES // N_REP
    far_box = jnp.clip(near_home // N_REP + jax.random.randint(jax.random.fold_in(key, 107), shape, -1, 2), 0, box_total - 1)
    far_home = far_box * N_REP + jax.random.randint(jax.random.fold_in(key, 108), shape, 0, N_REP)
    far_col = jax.random.randint(jax.random.fold_in(key, 109), shape, 0, 1 << 16) % counts[far_home, plane_ids, receiver]
    return jnp.stack([near_home * CAP + near_col, far_home * CAP + far_col], axis=-1).astype(jnp.int32)


def draw_pair_count(key, part):
    first_draw = jax.random.randint(jax.random.fold_in(key, 21), (HOMES * N_SUB,), 0, PAIRS_DEV)
    second_draw = jax.random.randint(jax.random.fold_in(key, 22), (HOMES * N_SUB,), 0, PAIRS_DEV)
    counts = 1 + first_draw * second_draw // PAIRS_DEV
    busiest = jax.random.randint(jax.random.fold_in(key, 23), (), 0, HOMES * N_SUB)
    counts = jnp.where(jnp.arange(HOMES * N_SUB) == busiest, PAIRS_DEV, counts)
    return counts.reshape(HOMES, N_SUB).astype(jnp.int32)


def draw_tile_info(key, part):
    present = jax.random.randint(jax.random.fold_in(key, 31), (HOMES, HT), TILE // 2, TILE + 1)
    fullest = jax.random.randint(jax.random.fold_in(key, 32), (HOMES,), 0, HT)
    present = jnp.where(jnp.arange(HT)[None, :] == fullest[:, None], TILE, present)
    run_length = jax.random.randint(jax.random.fold_in(key, 33), (HOMES, HT), 1, 5)
    return jnp.stack([present, run_length], axis=-1).astype(jnp.int32)


def draw_atom_data(key, part):
    unit_cube = jax.random.uniform(jax.random.fold_in(key, 1), (HOMES, HT, 3, TILE), jnp.float32)
    home_ids = jnp.arange(HOMES)
    box_of = (home_ids // N_REP).astype(jnp.float32)[:, None, None]
    rep_of = (home_ids % N_REP).astype(jnp.float32)[:, None, None]
    coord_x = 32.0 * unit_cube[:, :, 0]
    coord_y = 16.0 * (rep_of + unit_cube[:, :, 1])
    coord_z = 16.0 * (box_of + unit_cube[:, :, 2])
    charge = jax.random.uniform(jax.random.fold_in(key, 2), (HOMES, HT, TILE), jnp.float32, -0.8, 0.8)
    return jnp.stack([coord_x, coord_y, coord_z, charge], axis=2).astype(jnp.float32)


def set_ends(values, key, smallest, high):
    place = [jax.random.randint(jax.random.fold_in(key, axis), (), 0, length) for axis, length in enumerate(values.shape)]
    widest = values.shape.index(max(values.shape))
    beside = place[:widest] + [(place[widest] + 1) % values.shape[widest]] + place[widest + 1:]
    return values.at[tuple(place)].set(smallest).at[tuple(beside)].set(high)


def setup_inputs(seed: int = 0, part: int = 0) -> dict:
    keys = jax.random.split(jax.random.key(seed), 10)
    own_keys = jax.random.split(jax.random.fold_in(keys[9], part), 10)
    atom_data = draw_atom_data(jax.random.fold_in(jax.random.fold_in(keys[9], part), 71), part)
    atom_type = set_ends(jax.random.randint(own_keys[1], (HOMES, HT, TILE), 0, NTYPE), jax.random.fold_in(own_keys[1], 1), 0, NTYPE - 1).astype(jnp.int32)
    tile_info = draw_tile_info(jax.random.fold_in(jax.random.fold_in(keys[9], part), 71), part)
    lj_repulsion = jnp.clip(jnp.exp(jax.random.uniform(keys[3], (NTYPE,), jnp.float32, math.log(100.0), math.log(1000.0))), 100.0, 1000.0)
    lj_dispersion = jnp.clip(jnp.exp(jax.random.uniform(keys[4], (NTYPE,), jnp.float32, math.log(3.0), math.log(30.0))), 3.0, 30.0)
    send_tiles = draw_send_tiles(jax.random.fold_in(jax.random.fold_in(keys[9], part), 71), part)
    send_count = draw_send_count(jax.random.fold_in(jax.random.fold_in(keys[9], part), 71), part)
    pair_slots = draw_pair_slots(jax.random.fold_in(jax.random.fold_in(keys[9], part), 71), part)
    pair_count = draw_pair_count(jax.random.fold_in(jax.random.fold_in(keys[9], part), 71), part)
    return {"atom_data": atom_data, "atom_type": atom_type, "tile_info": tile_info, "lj_repulsion": lj_repulsion, "lj_dispersion": lj_dispersion, "send_tiles": send_tiles, "send_count": send_count, "pair_slots": pair_slots, "pair_count": pair_count}


COULOMB = 332.0636
SOFTENING = 9.0
CUTOFF_SQ = 144.0

def pair_forces(near_tile, far_tile, same_tile, near_info, far_info):
    atom_ids = jnp.arange(near_tile.shape[-1], dtype=jnp.int32)
    near_live = atom_ids[None, :] < near_info[:, 0:1]
    far_live = atom_ids[None, :] < far_info[:, 0:1]
    near_mol = atom_ids[None, :] // near_info[:, 1:2]
    far_mol = atom_ids[None, :] // far_info[:, 1:2]
    bonded = same_tile[:, None, None] & (near_mol[:, :, None] == far_mol[:, None, :])
    keeper = near_live[:, :, None] & far_live[:, None, :] & jnp.logical_not(bonded)
    separation = near_tile[:, 0:3, :, None] - far_tile[:, 0:3, None, :]
    dist_sq = lax.optimization_barrier(jnp.sum(separation * separation, axis=1))
    inverse = 1.0 / (dist_sq + SOFTENING)
    inv_cube = inverse * inverse * inverse
    repulsion = near_tile[:, 4, :, None] * far_tile[:, 4, None, :]
    attract = near_tile[:, 5, :, None] * far_tile[:, 5, None, :]
    charges = COULOMB * near_tile[:, 3, :, None] * far_tile[:, 3, None, :]
    rooted = jnp.sqrt(inverse)
    energy = repulsion * inv_cube * inv_cube - attract * inv_cube + charges * rooted
    derivative = (-6.0 * repulsion * inv_cube * inv_cube + 3.0 * attract * inv_cube - 0.5 * charges * rooted) * inverse
    window = jnp.maximum(1.0 - dist_sq / CUTOFF_SQ, 0.0)
    gradient = window * window * derivative - 2.0 / CUTOFF_SQ * window * energy
    weight = jnp.where(keeper, -2.0 * gradient, 0.0)
    return lax.optimization_barrier(jnp.sum(weight[:, None] * separation, axis=-1))

def reference(atom_data, atom_type, tile_info, lj_repulsion, lj_dispersion, send_tiles, send_count, pair_slots, pair_count):
    home_total = atom_data.shape[0]
    tiles_home = atom_data.shape[1]
    tile_width = atom_data.shape[3]
    planes = send_tiles.shape[1]
    capacity = send_tiles.shape[3]
    pairs_each = pair_slots.shape[2]
    repulsion = lj_repulsion[atom_type]
    dispersion = lj_dispersion[atom_type]
    record = jnp.concatenate([atom_data, repulsion[:, :, None], dispersion[:, :, None]], axis=2)
    record = record.reshape(home_total * tiles_home, 6, tile_width)
    tile_meta = tile_info.reshape(home_total * tiles_home, 2)
    receiver = jnp.arange(home_total, dtype=jnp.int32)[:, None, None]
    plane_ids = jnp.arange(planes, dtype=jnp.int32)[None, :, None]

    def locate(slot):
        source = slot // capacity
        column = slot % capacity
        tile_ids = source * tiles_home + send_tiles[source, plane_ids, receiver, column]
        shipped = column < send_count[source, plane_ids, receiver]
        return (tile_ids.astype(jnp.int32), shipped)
    near_slot = pair_slots[..., 0]
    far_slot = pair_slots[..., 1]
    near_ids, near_sent = locate(near_slot)
    far_ids, far_sent = locate(far_slot)
    same_tile = near_slot == far_slot
    active = jnp.arange(pairs_each, dtype=jnp.int32)[None, None, :] < pair_count[:, :, None]

    def flatten(array):
        return array.reshape(home_total * planes, pairs_each)

    def device_pairs(packed):
        near_ids, far_ids, near_sent, far_sent, same_tile, active = packed
        near_meta = jnp.stack([tile_meta[near_ids, 0] * near_sent.astype(jnp.int32), tile_meta[near_ids, 1]], axis=-1)
        far_meta = jnp.stack([tile_meta[far_ids, 0] * far_sent.astype(jnp.int32), tile_meta[far_ids, 1]], axis=-1)
        result = pair_forces(record[near_ids], record[far_ids], same_tile, near_meta, far_meta)
        return jnp.where(active[:, None, None], result, 0.0)
    packed = (flatten(near_ids), flatten(far_ids), flatten(near_sent), flatten(far_sent), flatten(same_tile), flatten(active))
    contributions = lax.map(device_pairs, packed)
    summed = jnp.zeros((home_total * tiles_home, 3, tile_width), jnp.float32)
    summed = summed.at[near_ids.reshape(-1)].add(contributions.reshape(-1, 3, tile_width))
    return summed.reshape(home_total, tiles_home, 3, tile_width)
```

```python
import functools

import jax
import jax.numpy as jnp
from jax import lax
from jax.experimental import pallas as pl
from jax.experimental.pallas import tpu as pltpu
from jax.sharding import PartitionSpec as P

COULOMB = 332.0636
SOFTENING = 9.0
CUTOFF_SQ = 144.0
MESH = pl.DeviceIdType.MESH
FIELDS = 8
CHUNK = 32
VMEM = pltpu.VMEM
SMEM = pltpu.SMEM


def spec(space):
    return pl.BlockSpec(memory_space=space)


def pack_kernel(data_ref, type_ref, info_ref, rep_ref, dis_ref, send_ref, count_ref, out_ref, rep_rows, dis_rows):
    kinds = type_ref[...]
    repulsion = jnp.zeros(kinds.shape, jnp.float32)
    dispersion = jnp.zeros(kinds.shape, jnp.float32)
    for kind in range(rep_ref.shape[0]):
        match = kinds == kind
        repulsion = jnp.where(match, rep_ref[kind], repulsion)
        dispersion = jnp.where(match, dis_ref[kind], dispersion)
    rep_rows[...] = repulsion
    dis_rows[...] = dispersion
    homes, capacity = send_ref.shape
    width = data_ref.shape[2]
    lane = lax.broadcasted_iota(jnp.int32, (1, width), 1)
    middle = lane.astype(jnp.float32) + 0.5

    def fill(home, _):
        for column in range(capacity):
            tile = send_ref[home, column]
            present = jnp.where(column < count_ref[0, home], info_ref[tile, 0], 0)
            live = lane < present
            run = jnp.full((1, width), info_ref[tile, 1], jnp.int32).astype(jnp.float32)
            atoms = data_ref[tile]
            out_ref[home, column, 0:3] = atoms[0:3]
            out_ref[home, column, 3:4] = jnp.where(live, atoms[3:4], 0.0)
            out_ref[home, column, 4:5] = jnp.where(live, rep_rows[pl.ds(tile, 1)], 0.0)
            out_ref[home, column, 5:6] = jnp.where(live, dis_rows[pl.ds(tile, 1)], 0.0)
            out_ref[home, column, 6:7] = jnp.floor(middle / run)
            out_ref[home, column, 7:8] = jnp.zeros((1, width), jnp.float32)
        return 0

    lax.fori_loop(0, homes, fill, 0, unroll=homes <= 8)


def pack(data, kinds, info, repulsion, dispersion, chosen, counts):
    homes, capacity = chosen.shape
    tiles, _, width = data.shape
    return pl.pallas_call(
        pack_kernel,
        out_shape=jax.ShapeDtypeStruct((homes, capacity, FIELDS, width), jnp.float32),
        in_specs=[spec(VMEM), spec(VMEM)] + [spec(SMEM)] * 5,
        out_specs=spec(VMEM),
        scratch_shapes=[VMEM((tiles, width), jnp.float32)] * 2,
    )(data, kinds, info, repulsion, dispersion, chosen, counts)


def distinct_pairs(pair_list, pair_total, slot_total):
    pair_max = pair_list.shape[0]
    near, far = pair_list[:, 0], pair_list[:, 1]
    rank = jnp.arange(pair_max, dtype=jnp.int32)
    active = rank < pair_total
    forward = near <= far
    code = jnp.maximum(near, far) * slot_total + jnp.minimum(near, far)
    code = jnp.where(active, code, slot_total * slot_total)
    same = (code[:, None] == code[None, :]) & active[None, :]
    tally = jnp.sum(jnp.where(same, jnp.where(forward, 256, 1)[None, :], 0), axis=1)
    earlier = jnp.sum(jnp.where(same & (rank[None, :] < rank[:, None]), 1, 0), axis=1)
    first = active & (earlier == 0)
    place = jnp.sum(jnp.where(first[None, :] & (code[None, :] < code[:, None]), 1, 0), axis=1)
    hit = (place[None, :] == rank[:, None]) & first[None, :]
    codes = jnp.sum(jnp.where(hit, code[None, :], 0), axis=1)
    tallies = jnp.sum(jnp.where(hit, tally[None, :], 0), axis=1)
    used = jnp.sum(first.astype(jnp.int32))
    return jnp.stack([codes, tallies]), used.reshape(1)


def force_kernel(list_ref, used_ref, rec_ref, out_ref, far_ref, back_ref, slot_ref):
    slots, _, width = rec_ref.shape
    homes = out_ref.shape[0]
    capacity = slots // homes
    scale = 1.0 / (CUTOFF_SQ * CUTOFF_SQ)
    diag = lax.broadcasted_iota(jnp.int32, (width, width), 0) == lax.broadcasted_iota(jnp.int32, (width, width), 1)

    def clear(slot, _):
        slot_ref[slot] = jnp.zeros(slot_ref.shape[1:], jnp.float32)
        return 0

    lax.fori_loop(0, slots, clear, 0)

    def open_group(far):
        turned = jnp.transpose(rec_ref[far])
        for field in range(7):
            far_ref[field] = jnp.broadcast_to(turned[:, field : field + 1], (width, width))
        back_ref[...] = jnp.zeros(back_ref.shape, jnp.float32)

    def close_group(far):
        for axis in range(3):
            column = jnp.sum(back_ref[axis], axis=1, keepdims=True)
            spread = jnp.where(diag, column, 0.0)
            folded = jnp.sum(spread.reshape(width // 8, 8, width), axis=0)
            slot_ref[far, axis] = slot_ref[far, axis] - folded

    def tile_pair(near, forward, backward, own, both):
        rows = rec_ref[near]
        x, y, z = rows[0:1], rows[1:2], rows[2:3]
        charge = rows[3:4] * (COULOMB * scale)
        rep = rows[4:5] * (12.0 * scale)
        dis = rows[5:6] * (6.0 * scale)
        mol = rows[6:7]
        sums = [jnp.zeros((8, width), jnp.float32) for _ in range(3)]
        for start in range(0, width, CHUNK):
            at = slice(start, start + CHUNK)
            dx = x - far_ref[0, at]
            dy = y - far_ref[1, at]
            dz = z - far_ref[2, at]
            soft = dx * dx + dy * dy + (dz * dz + SOFTENING)
            root = lax.rsqrt(soft)
            inverse = root * root
            cube = inverse * inverse * inverse
            window = jnp.maximum((CUTOFF_SQ + SOFTENING) - soft, 0.0)
            part = window * inverse
            first = (rep * far_ref[4, at]) * cube * (part + 1.0 / 3.0)
            second = (dis * far_ref[5, at]) * (part + 2.0 / 3.0)
            third = (charge * far_ref[3, at]) * root * (part + 4.0)
            weight = ((first - second) * cube + third) * window
            if own:
                weight = jnp.where(mol == far_ref[6, at], 0.0, weight)
            for axis, step in enumerate((dx, dy, dz)):
                term = weight * step
                sums[axis] = sums[axis] + jnp.sum(term.reshape(CHUNK // 8, 8, width), axis=0)
                if both:
                    back_ref[axis, at] = back_ref[axis, at] + term * backward
        for axis in range(3):
            slot_ref[near, axis] = slot_ref[near, axis] + sums[axis] * forward

    used = used_ref[0]

    def visit(index, open_slot):
        code = list_ref[0, index]
        tally = list_ref[1, index]
        far = code // slots
        near = code - far * slots
        forward_count = tally >> 8
        backward_count = tally & 255
        forward = forward_count.astype(jnp.float32)
        backward = backward_count.astype(jnp.float32)

        @pl.when(far != open_slot)
        def _():
            @pl.when(open_slot >= 0)
            def _():
                close_group(open_slot)

            open_group(far)

        own = near == far
        both = backward_count > 0

        @pl.when(own)
        def _():
            tile_pair(near, forward, backward, True, False)

        @pl.when(jnp.logical_not(own) & both)
        def _():
            tile_pair(near, forward, backward, False, True)

        @pl.when(jnp.logical_not(own) & jnp.logical_not(both))
        def _():
            tile_pair(near, forward, backward, False, False)

        return far

    last = lax.fori_loop(0, used, visit, jnp.int32(-1))

    @pl.when(last >= 0)
    def _():
        close_group(last)

    def finish(home, _):
        rows = []
        for column in range(capacity):
            for axis in range(3):
                rows.append(jnp.sum(slot_ref[home * capacity + column, axis], axis=0, keepdims=True))
        for row, value in enumerate(rows):
            out_ref[home, row : row + 1] = value
        for row in range(len(rows), out_ref.shape[1]):
            out_ref[home, row : row + 1] = jnp.zeros((1, width), jnp.float32)
        return 0

    lax.fori_loop(0, homes, finish, 0)


def block_rows(capacity):
    return -(-3 * capacity // 8) * 8


def slot_forces(listed, used, rec, homes):
    slots, _, width = rec.shape
    rows = block_rows(slots // homes)
    return pl.pallas_call(
        force_kernel,
        out_shape=jax.ShapeDtypeStruct((homes, rows, width), jnp.float32),
        in_specs=[spec(SMEM), spec(SMEM), spec(VMEM)],
        out_specs=spec(VMEM),
        scratch_shapes=[
            VMEM((7, width, width), jnp.float32),
            VMEM((3, width, width), jnp.float32),
            VMEM((slots, 3, 8, width), jnp.float32),
        ],
    )(listed, used, rec)


def box_rep(home, reps):
    return {"box": home // reps, "rep": lax.rem(home, reps)}


def exchange_kernel(out_ref, ids_ref, in_ref, all_ids_ref, got, got_ids, send_sem, recv_sem, id_send, id_recv):
    homes = out_ref.shape[0]
    subs = all_ids_ref.shape[0]
    reps = lax.axis_size("rep")
    me = lax.axis_index("box") * reps + lax.axis_index("rep")
    sub = lax.axis_index("sub")
    barrier = pltpu.get_barrier_semaphore()

    def greet(step, _):
        peer = lax.rem(me + step, homes)
        pl.semaphore_signal(barrier, inc=1, device_id=box_rep(peer, reps), device_id_type=MESH)
        return 0

    def greet_sub(step, _):
        pl.semaphore_signal(barrier, inc=1, device_id={"sub": lax.rem(sub + step, subs)}, device_id_type=MESH)
        return 0

    lax.fori_loop(1, homes, greet, 0, unroll=homes <= 8)
    lax.fori_loop(1, subs, greet_sub, 0, unroll=True)
    pl.semaphore_wait(barrier, homes - 1 + subs - 1)

    def to_home(step):
        peer = lax.rem(me + step, homes)
        return pltpu.make_async_remote_copy(
            src_ref=out_ref.at[peer],
            dst_ref=got.at[step],
            send_sem=send_sem.at[step],
            recv_sem=recv_sem.at[step],
            device_id=box_rep(peer, reps),
            device_id_type=MESH,
        )

    def to_sub(step):
        return pltpu.make_async_remote_copy(
            src_ref=ids_ref,
            dst_ref=got_ids.at[step],
            send_sem=id_send.at[step],
            recv_sem=id_recv.at[step],
            device_id={"sub": lax.rem(sub + step, subs)},
            device_id_type=MESH,
        )

    def start(step, _):
        to_home(step).start()
        return 0

    def start_sub(step, _):
        to_sub(step).start()
        return 0

    lax.fori_loop(1, homes, start, 0, unroll=homes <= 8)
    lax.fori_loop(1, subs, start_sub, 0, unroll=True)
    in_ref[me] = out_ref[me]
    all_ids_ref[sub] = ids_ref[...]

    def finish(step, _):
        to_home(step).wait()
        in_ref[lax.rem(me + homes - step, homes)] = got[step]
        return 0

    def finish_sub(step, _):
        to_sub(step).wait()
        all_ids_ref[lax.rem(sub + subs - step, subs)] = got_ids[step]
        return 0

    lax.fori_loop(1, homes, finish, 0, unroll=homes <= 8)
    lax.fori_loop(1, subs, finish_sub, 0, unroll=True)


def exchange(outgoing, ids, subs):
    homes = outgoing.shape[0]
    return pl.pallas_call(
        exchange_kernel,
        out_shape=(
            jax.ShapeDtypeStruct(outgoing.shape, jnp.float32),
            jax.ShapeDtypeStruct((subs,) + ids.shape, jnp.float32),
        ),
        in_specs=[spec(VMEM), spec(VMEM)],
        out_specs=(spec(VMEM), spec(VMEM)),
        scratch_shapes=[
            VMEM(outgoing.shape, jnp.float32),
            VMEM((subs,) + ids.shape, jnp.float32),
            pltpu.SemaphoreType.DMA((homes,)),
            pltpu.SemaphoreType.DMA((homes,)),
            pltpu.SemaphoreType.DMA((subs,)),
            pltpu.SemaphoreType.DMA((subs,)),
        ],
        compiler_params=pltpu.CompilerParams(collective_id=0, has_side_effects=True),
    )(outgoing, ids)


def return_kernel(force_ref, ids_ref, out_ref, got, send_sem, recv_sem):
    homes, rows, width = force_ref.shape
    subs = ids_ref.shape[0]
    reps = lax.axis_size("rep")
    me = lax.axis_index("box") * reps + lax.axis_index("rep")
    sub = lax.axis_index("sub")
    total = subs * homes
    mine = sub * homes + me
    barrier = pltpu.get_barrier_semaphore()

    def place(step):
        peer = lax.rem(mine + step, total)
        home = lax.rem(peer, homes)
        return home, {"sub": peer // homes, "box": home // reps, "rep": lax.rem(home, reps)}

    def greet(step, _):
        pl.semaphore_signal(barrier, inc=1, device_id=place(step)[1], device_id_type=MESH)
        return 0

    lax.fori_loop(1, total, greet, 0, unroll=total <= 16)
    pl.semaphore_wait(barrier, total - 1)

    def copy(step):
        home, device = place(step)
        return pltpu.make_async_remote_copy(
            src_ref=force_ref.at[home],
            dst_ref=got.at[mine],
            send_sem=send_sem.at[step],
            recv_sem=recv_sem.at[step],
            device_id=device,
            device_id_type=MESH,
        )

    def start(step, _):
        copy(step).start()
        return 0

    def finish(step, _):
        copy(step).wait()
        return 0

    lax.fori_loop(1, total, start, 0, unroll=total <= 16)
    got[mine] = force_ref[me]
    lax.fori_loop(1, total, finish, 0, unroll=total <= 16)
    held = out_ref.shape[0]
    wanted = lax.broadcasted_iota(jnp.int32, (held, homes * rows), 0) + sub * held
    wanted = wanted.astype(jnp.float32)
    result = jnp.zeros((held, width), jnp.float32)
    for plane in range(subs):
        pick = (ids_ref[plane, 0:1] == wanted).astype(jnp.float32)
        block = got[plane * homes : (plane + 1) * homes].reshape(homes * rows, width)
        result = result + jnp.dot(
            pick, block, precision=lax.Precision.HIGHEST, preferred_element_type=jnp.float32
        )
    out_ref[...] = result


def send_back(forces, ids, held):
    homes, rows, width = forces.shape
    subs = ids.shape[0]
    return pl.pallas_call(
        return_kernel,
        out_shape=jax.ShapeDtypeStruct((held, width), jnp.float32),
        in_specs=[spec(VMEM), spec(VMEM)],
        out_specs=spec(VMEM),
        scratch_shapes=[
            VMEM((subs * homes, rows, width), jnp.float32),
            pltpu.SemaphoreType.DMA((subs * homes,)),
            pltpu.SemaphoreType.DMA((subs * homes,)),
        ],
        compiler_params=pltpu.CompilerParams(collective_id=1, has_side_effects=True),
    )(forces, ids)


def row_ids(chosen):
    homes, capacity = chosen.shape
    rows = block_rows(capacity)
    ids = (3 * chosen[:, :, None] + jnp.arange(3, dtype=jnp.int32)).reshape(homes, 3 * capacity)
    ids = jnp.pad(ids, ((0, 0), (0, rows - 3 * capacity)), constant_values=-1)
    return jnp.broadcast_to(ids.reshape(1, homes * rows).astype(jnp.float32), (8, homes * rows))


def per_device(
    atom_data, atom_type, tile_info, lj_repulsion, lj_dispersion, send_tiles, send_count, pair_slots, pair_count
):
    subs = lax.axis_size("sub")
    tiles, width = atom_data.shape[1], atom_data.shape[3]
    chosen = send_tiles[0, 0]
    homes, capacity = chosen.shape
    slots = homes * capacity
    outgoing = pack(atom_data[0], atom_type[0], tile_info[0], lj_repulsion, lj_dispersion, chosen, send_count[0])
    listed, used = distinct_pairs(pair_slots[0, 0], pair_count[0, 0], slots)
    incoming, ids = exchange(outgoing, row_ids(chosen), subs)
    forces = slot_forces(listed, used, incoming.reshape(slots, FIELDS, width), homes)
    held = tiles // subs
    return send_back(forces, ids, 3 * held).reshape(1, held, 3, width)


def solution(mesh):
    placed = (
        P(("groups", "box", "rep"), None, None, None),
        P(("groups", "box", "rep"), None, None),
        P(("groups", "box", "rep"), None, None),
        P(),
        P(),
        P(("groups", "box", "rep"), "sub", None, None),
        P(("groups", "box", "rep"), "sub", None),
        P(("groups", "box", "rep"), "sub", None, None),
        P(("groups", "box", "rep"), "sub"),
    )
    return jax.shard_map(
        per_device,
        mesh=mesh,
        in_specs=placed,
        out_specs=P(("groups", "box", "rep"), "sub", None, None),
        check_vma=False,
    )
```

```python
import functools

import jax
import jax.numpy as jnp
from jax import lax
from jax.experimental import pallas as pl
from jax.experimental.pallas import tpu as pltpu
from jax.sharding import PartitionSpec as P

COULOMB = 332.0636
SOFTENING = 9.0
CUTOFF_SQ = 144.0
MESH = pl.DeviceIdType.MESH
FIELDS = 5
CHUNK = 32
FAR_SHIFT = 12
VMEM = pltpu.VMEM
SMEM = pltpu.SMEM


def spec(space):
    return pl.BlockSpec(memory_space=space)


def padded(rows):
    return -(-rows // 8) * 8


def box_rep(home, reps):
    return {"box": home // reps, "rep": lax.rem(home, reps)}


def list_pairs(pair_ref, pair_total, list_ref):
    pair_max = list_ref.shape[1]
    shape = (pair_max, pair_max)
    down = lax.broadcasted_iota(jnp.int32, shape, 0)
    along = lax.broadcasted_iota(jnp.int32, shape, 1)
    near, far = pair_ref[0, 0, 0:1], pair_ref[0, 0, 1:2]
    active_row = (along[0:1] < pair_total).astype(jnp.int32)
    active = (down[:, 0:1] < pair_total).astype(jnp.int32)
    code_row = jnp.maximum(near, far) * (1 << FAR_SHIFT) + jnp.minimum(near, far)
    code_row = jnp.where(active_row > 0, code_row, -1)
    mark_row = jnp.where(near <= far, 256, 1) * active_row

    def across(values):
        return jnp.sum(values.astype(jnp.float32), axis=1, keepdims=True).astype(jnp.int32)

    code = across(jnp.where(down == along, code_row, 0))
    same = code == code_row
    tally = across(jnp.where(same, mark_row, 0))
    earlier = across(jnp.where(same, jnp.where(along < down, 1, 0), 0))
    first = jnp.where(earlier == 0, active, 0)
    first_row = jnp.sum(jnp.where(down == along, first, 0), axis=0, keepdims=True)
    place = across(jnp.where(code_row < code, first_row, 0))
    place = jnp.where(first > 0, place, -1)
    hit = place == along
    list_ref[0:1] = jnp.sum(jnp.where(hit, code, 0), axis=0, keepdims=True)
    list_ref[1:2] = jnp.sum(jnp.where(hit, tally, 0), axis=0, keepdims=True)
    list_ref[2:3] = jnp.sum(jnp.broadcast_to(first, shape), axis=0, keepdims=True)


def exchange_kernel(
    data_ref, type_ref, info_ref, send_ref, count_ref, pair_ref, total_ref,
    in_ref, all_ids_ref, list_ref,
    packed, ids, got, got_ids, send_sem, recv_sem, id_send, id_recv,
):
    homes, rows, width = in_ref.shape
    capacity = send_ref.shape[1]
    subs = all_ids_ref.shape[0]
    back_rows = ids.shape[1] // homes
    reps = lax.axis_size("rep")
    me = lax.axis_index("box") * reps + lax.axis_index("rep")
    sub = lax.axis_index("sub")
    barrier = pltpu.get_barrier_semaphore()
    unroll = homes <= 8

    def greet(step, _):
        peer = lax.rem(me + step, homes)
        pl.semaphore_signal(barrier, inc=1, device_id=box_rep(peer, reps), device_id_type=MESH)
        return 0

    def greet_sub(step, _):
        pl.semaphore_signal(barrier, inc=1, device_id={"sub": lax.rem(sub + step, subs)}, device_id_type=MESH)
        return 0

    lax.fori_loop(1, homes, greet, 0, unroll=unroll)
    lax.fori_loop(1, subs, greet_sub, 0, unroll=True)

    lane = lax.broadcasted_iota(jnp.int32, (1, width), 1)
    id_lane = lax.broadcasted_iota(jnp.int32, (1, ids.shape[1]), 1)

    def fill(home, row_ids):
        runs = jnp.zeros((1, width), jnp.int32)
        for column in range(capacity):
            tile = send_ref[0, column, 0, home]
            present = jnp.where(column < count_ref[0, 0, home], info_ref[0, 0, tile], 0)
            live = lane < present
            atoms = data_ref[0, tile]
            base = FIELDS * column
            packed[home, base : base + 3] = atoms[0:3]
            packed[home, base + 3 : base + 4] = jnp.where(live, atoms[3:4], 0.0)
            kinds = jnp.where(live, type_ref[0, pl.ds(tile, 1)], -1)
            packed[home, base + 4 : base + 5] = kinds.astype(jnp.float32)
            runs = jnp.where(lane == column, info_ref[0, 1, tile], runs)
            place = id_lane - (home * back_rows + 3 * column)
            row_ids = jnp.where((place >= 0) & (place < 3), 3 * tile + place, row_ids)
        base = FIELDS * capacity
        packed[home, base : base + 1] = runs.astype(jnp.float32)
        for row in range(base + 1, rows):
            packed[home, row : row + 1] = jnp.zeros((1, width), jnp.float32)
        return row_ids

    row_ids = lax.fori_loop(0, homes, fill, jnp.full(id_lane.shape, -1, jnp.int32), unroll=unroll)
    ids[...] = jnp.broadcast_to(row_ids.astype(jnp.float32), ids.shape)
    pl.semaphore_wait(barrier, homes - 1 + subs - 1)

    def to_home(step):
        peer = lax.rem(me + step, homes)
        return pltpu.make_async_remote_copy(
            src_ref=packed.at[peer],
            dst_ref=got.at[step],
            send_sem=send_sem.at[step],
            recv_sem=recv_sem.at[step],
            device_id=box_rep(peer, reps),
            device_id_type=MESH,
        )

    def to_sub(step):
        return pltpu.make_async_remote_copy(
            src_ref=ids,
            dst_ref=got_ids.at[step],
            send_sem=id_send.at[step],
            recv_sem=id_recv.at[step],
            device_id={"sub": lax.rem(sub + step, subs)},
            device_id_type=MESH,
        )

    def start(step, _):
        to_home(step).start()
        return 0

    def start_sub(step, _):
        to_sub(step).start()
        return 0

    lax.fori_loop(1, homes, start, 0, unroll=unroll)
    lax.fori_loop(1, subs, start_sub, 0, unroll=True)
    in_ref[me] = packed[me]
    all_ids_ref[sub] = ids[...]
    list_pairs(pair_ref, total_ref[0, 0], list_ref)

    def finish(step, _):
        to_home(step).wait()
        in_ref[lax.rem(me + homes - step, homes)] = got[step]
        return 0

    def finish_sub(step, _):
        to_sub(step).wait()
        all_ids_ref[lax.rem(sub + subs - step, subs)] = got_ids[step]
        return 0

    lax.fori_loop(1, homes, finish, 0, unroll=unroll)
    lax.fori_loop(1, subs, finish_sub, 0, unroll=True)


def exchange(data, kinds, info, chosen, counts, pairs, totals, subs):
    homes, capacity = chosen.shape[2:]
    width = data.shape[3]
    block = (homes, padded(FIELDS * capacity + 1), width)
    id_block = (8, homes * padded(3 * capacity))
    return pl.pallas_call(
        exchange_kernel,
        out_shape=(
            jax.ShapeDtypeStruct(block, jnp.float32),
            jax.ShapeDtypeStruct((subs,) + id_block, jnp.float32),
            jax.ShapeDtypeStruct((3, pairs.shape[2]), jnp.int32),
        ),
        in_specs=[spec(VMEM), spec(VMEM), spec(SMEM), spec(SMEM), spec(SMEM), spec(VMEM), spec(SMEM)],
        out_specs=(spec(VMEM),) * 3,
        scratch_shapes=[
            VMEM(block, jnp.float32),
            VMEM(id_block, jnp.float32),
            VMEM(block, jnp.float32),
            VMEM((subs,) + id_block, jnp.float32),
            pltpu.SemaphoreType.DMA((homes,)),
            pltpu.SemaphoreType.DMA((homes,)),
            pltpu.SemaphoreType.DMA((subs,)),
            pltpu.SemaphoreType.DMA((subs,)),
        ],
        compiler_params=pltpu.CompilerParams(collective_id=0, has_side_effects=True),
    )(
        data,
        kinds,
        jnp.transpose(info, (0, 2, 1)),
        jnp.transpose(chosen, (0, 3, 1, 2)),
        counts,
        jnp.transpose(pairs, (0, 1, 3, 2)),
        totals,
    )


def force_kernel(list_ref, rep_ref, dis_ref, in_ref, out_ref, kind_ref, rec_ref, far_ref, back_ref, slot_ref):
    slots, width = kind_ref.shape
    homes = out_ref.shape[0]
    capacity = slots // homes
    scale = 1.0 / (CUTOFF_SQ * CUTOFF_SQ)
    diag = lax.broadcasted_iota(jnp.int32, (width, width), 0) == lax.broadcasted_iota(jnp.int32, (width, width), 1)
    lane = lax.broadcasted_iota(jnp.int32, (1, width), 1)
    atom_row = lane.astype(jnp.float32) + 0.5

    def unpack(home, _):
        runs = in_ref[home, FIELDS * capacity : FIELDS * capacity + 1]
        for column in range(capacity):
            slot = home * capacity + column
            base = FIELDS * column
            rec_ref[slot, 0:4] = in_ref[home, base : base + 4]
            kind_ref[pl.ds(slot, 1)] = in_ref[home, base + 4 : base + 5]
            run = jnp.sum(jnp.where(lane == column, runs, 0.0), axis=1, keepdims=True)
            rec_ref[slot, 6:7] = jnp.broadcast_to(1.0 / run, (1, width))
            slot_ref[slot] = jnp.zeros(slot_ref.shape[1:], jnp.float32)
        return 0

    lax.fori_loop(0, homes, unpack, 0, unroll=homes <= 8)
    slot_ref[slots] = jnp.zeros(slot_ref.shape[1:], jnp.float32)
    kinds = kind_ref[...]
    repulsion = jnp.zeros(kinds.shape, jnp.float32)
    dispersion = jnp.zeros(kinds.shape, jnp.float32)
    for kind in range(rep_ref.shape[0]):
        match = kinds == float(kind)
        repulsion = jnp.where(match, rep_ref[kind], repulsion)
        dispersion = jnp.where(match, dis_ref[kind], dispersion)
    rec_ref[:, 4] = repulsion
    rec_ref[:, 5] = dispersion
    back_ref[...] = jnp.zeros(back_ref.shape, jnp.float32)

    def close_group(far):
        for axis in range(3):
            column = jnp.sum(back_ref[axis], axis=1, keepdims=True)
            spread = jnp.where(diag, column, 0.0)
            folded = jnp.sum(spread.reshape(width // 8, 8, width), axis=0)
            slot_ref[far, axis] = slot_ref[far, axis] - folded

    def change_group(closed, far):
        rows = rec_ref[far]
        for field in range(6):
            column = jnp.sum(jnp.where(diag, rows[field : field + 1], 0.0), axis=1, keepdims=True)
            far_ref[field] = jnp.broadcast_to(column, (width, width))
        close_group(closed)
        back_ref[...] = jnp.zeros(back_ref.shape, jnp.float32)

    def tile_pair(near, near_scale, far_scale, own, both):
        rows = rec_ref[near]
        x, y, z = rows[0:1], rows[1:2], rows[2:3]
        charge = rows[3:4] * (far_scale * (COULOMB * scale))
        rep = rows[4:5] * (far_scale * (12.0 * scale))
        dis = rows[5:6] * (far_scale * (6.0 * scale))
        if own:
            per_run = rows[6:7]
            mol = jnp.floor(atom_row * per_run)
        sums = [jnp.zeros((8, width), jnp.float32) for _ in range(3)]
        for start in range(0, width, CHUNK):
            at = slice(start, start + CHUNK)
            dx = x - far_ref[0, at]
            dy = y - far_ref[1, at]
            dz = z - far_ref[2, at]
            soft = dx * dx + dy * dy + (dz * dz + SOFTENING)
            root = lax.rsqrt(soft)
            inverse = root * root
            cube = inverse * inverse * inverse
            window = jnp.maximum((CUTOFF_SQ + SOFTENING) - soft, 0.0)
            part = window * inverse
            first = (rep * far_ref[4, at]) * cube * (part + 1.0 / 3.0)
            second = (dis * far_ref[5, at]) * (part + 2.0 / 3.0)
            third = (charge * far_ref[3, at]) * root * (part + 4.0)
            weight = ((first - second) * cube + third) * window
            if own:
                atoms = lax.broadcasted_iota(jnp.int32, (CHUNK, width), 0).astype(jnp.float32) + (start + 0.5)
                weight = jnp.where(mol == jnp.floor(atoms * per_run), 0.0, weight)
            for axis, step in enumerate((dx, dy, dz)):
                term = weight * step
                sums[axis] = sums[axis] + jnp.sum(term.reshape(CHUNK // 8, 8, width), axis=0)
                if both:
                    back_ref[axis, at] = back_ref[axis, at] + term
        for axis in range(3):
            slot_ref[near, axis] = slot_ref[near, axis] + sums[axis] * near_scale

    used = list_ref[2, 0]

    def visit(index, open_slot):
        code = list_ref[0, index]
        tally = list_ref[1, index]
        far = code >> FAR_SHIFT
        near = code & ((1 << FAR_SHIFT) - 1)
        forward = (tally >> 8).astype(jnp.float32)
        backward_count = tally & 255
        backward = backward_count.astype(jnp.float32)

        @pl.when(far != open_slot)
        def _():
            change_group(open_slot, far)

        both = backward_count > 0

        @pl.when(both)
        def _():
            ratio = jnp.full((8, width), forward, jnp.float32) / jnp.full((8, width), backward, jnp.float32)
            tile_pair(near, ratio, backward, False, True)

        @pl.when(jnp.logical_not(both))
        def _():
            @pl.when(near == far)
            def _():
                tile_pair(near, forward, 1.0, True, False)

            @pl.when(near != far)
            def _():
                tile_pair(near, forward, 1.0, False, False)

        return far

    close_group(lax.fori_loop(0, used, visit, jnp.int32(slots)))

    def finish(home, _):
        for column in range(capacity):
            for axis in range(3):
                row = 3 * column + axis
                out_ref[home, row : row + 1] = jnp.sum(slot_ref[home * capacity + column, axis], axis=0, keepdims=True)
        for row in range(3 * capacity, out_ref.shape[1]):
            out_ref[home, row : row + 1] = jnp.zeros((1, width), jnp.float32)
        return 0

    lax.fori_loop(0, homes, finish, 0, unroll=homes <= 8)


def slot_forces(listed, repulsion, dispersion, incoming, capacity):
    homes, _, width = incoming.shape
    slots = homes * capacity
    return pl.pallas_call(
        force_kernel,
        out_shape=jax.ShapeDtypeStruct((homes, padded(3 * capacity), width), jnp.float32),
        in_specs=[spec(SMEM), spec(SMEM), spec(SMEM), spec(VMEM)],
        out_specs=spec(VMEM),
        scratch_shapes=[
            VMEM((slots, width), jnp.float32),
            VMEM((slots, 8, width), jnp.float32),
            VMEM((6, width, width), jnp.float32),
            VMEM((3, width, width), jnp.float32),
            VMEM((slots + 1, 3, 8, width), jnp.float32),
        ],
    )(listed, repulsion, dispersion, incoming)


def return_kernel(force_ref, ids_ref, out_ref, got, send_sem, recv_sem):
    homes, rows, width = force_ref.shape
    subs = ids_ref.shape[0]
    reps = lax.axis_size("rep")
    me = lax.axis_index("box") * reps + lax.axis_index("rep")
    sub = lax.axis_index("sub")
    total = subs * homes
    mine = sub * homes + me
    barrier = pltpu.get_barrier_semaphore()

    def place(step):
        peer = lax.rem(mine + step, total)
        home = lax.rem(peer, homes)
        return home, {"sub": peer // homes, "box": home // reps, "rep": lax.rem(home, reps)}

    def greet(step, _):
        pl.semaphore_signal(barrier, inc=1, device_id=place(step)[1], device_id_type=MESH)
        return 0

    lax.fori_loop(1, total, greet, 0, unroll=total <= 16)
    pl.semaphore_wait(barrier, total - 1)

    def copy(step):
        home, device = place(step)
        return pltpu.make_async_remote_copy(
            src_ref=force_ref.at[home],
            dst_ref=got.at[mine],
            send_sem=send_sem.at[step],
            recv_sem=recv_sem.at[step],
            device_id=device,
            device_id_type=MESH,
        )

    def start(step, _):
        copy(step).start()
        return 0

    def finish(step, _):
        copy(step).wait()
        return 0

    lax.fori_loop(1, total, start, 0, unroll=total <= 16)
    got[mine] = force_ref[me]
    lax.fori_loop(1, total, finish, 0, unroll=total <= 16)
    tiles = out_ref.shape[0]
    held = 3 * tiles
    wanted = lax.broadcasted_iota(jnp.int32, (held, homes * rows), 0) + sub * held
    wanted = wanted.astype(jnp.float32)
    result = jnp.zeros((held, width), jnp.float32)
    for plane in range(subs):
        pick = (ids_ref[plane, 0:1] == wanted).astype(jnp.float32)
        block = got[plane * homes : (plane + 1) * homes].reshape(homes * rows, width)
        result = result + jnp.dot(
            pick, block, precision=lax.Precision.HIGHEST, preferred_element_type=jnp.float32
        )
    for row in range(held):
        out_ref[row // 3, row % 3] = result[row : row + 1]


def send_back(forces, ids, held):
    homes, rows, width = forces.shape
    subs = ids.shape[0]
    return pl.pallas_call(
        return_kernel,
        out_shape=jax.ShapeDtypeStruct((held, 3, 1, width), jnp.float32),
        in_specs=[spec(VMEM), spec(VMEM)],
        out_specs=spec(VMEM),
        scratch_shapes=[
            VMEM((subs * homes, rows, width), jnp.float32),
            pltpu.SemaphoreType.DMA((subs * homes,)),
            pltpu.SemaphoreType.DMA((subs * homes,)),
        ],
        compiler_params=pltpu.CompilerParams(collective_id=1, has_side_effects=True),
    )(forces, ids)


def per_device(
    atom_data, atom_type, tile_info, lj_repulsion, lj_dispersion, send_tiles, send_count, pair_slots, pair_count
):
    subs = lax.axis_size("sub")
    incoming, ids, listed = exchange(
        atom_data, atom_type, tile_info, send_tiles, send_count, pair_slots, pair_count, subs
    )
    forces = slot_forces(listed, lj_repulsion, lj_dispersion, incoming, send_tiles.shape[3])
    result = send_back(forces, ids, atom_data.shape[1] // subs)
    return jnp.transpose(result, (2, 0, 1, 3))


def solution(mesh):
    placed = (
        P(("groups", "box", "rep"), None, None, None),
        P(("groups", "box", "rep"), None, None),
        P(("groups", "box", "rep"), None, None),
        P(),
        P(),
        P(("groups", "box", "rep"), "sub", None, None),
        P(("groups", "box", "rep"), "sub", None),
        P(("groups", "box", "rep"), "sub", None, None),
        P(("groups", "box", "rep"), "sub"),
    )
    return jax.shard_map(
        per_device,
        mesh=mesh,
        in_specs=placed,
        out_specs=P(("groups", "box", "rep"), "sub", None, None),
        check_vma=False,
    )
```

```python
import functools

import jax
import jax.numpy as jnp
from jax import lax
from jax.experimental import pallas as pl
from jax.experimental.pallas import tpu as pltpu
from jax.sharding import PartitionSpec as P

COULOMB = 332.0636
SOFTENING = 9.0
CUTOFF_SQ = 144.0
MESH = pl.DeviceIdType.MESH
FIELDS = 5
CHUNK = 32
FAR_SHIFT = 12
VMEM = pltpu.VMEM
SMEM = pltpu.SMEM


def spec(space):
    return pl.BlockSpec(memory_space=space)


def padded(rows):
    return -(-rows // 8) * 8


def box_rep(home, reps):
    return {"box": home // reps, "rep": lax.rem(home, reps)}


def list_pairs(pair_ref, pair_total, list_ref):
    pair_max = list_ref.shape[1]
    shape = (pair_max, pair_max)
    down = lax.broadcasted_iota(jnp.int32, shape, 0)
    along = lax.broadcasted_iota(jnp.int32, shape, 1)
    near, far = pair_ref[0, 0, 0:1], pair_ref[0, 0, 1:2]
    active_row = (along[0:1] < pair_total).astype(jnp.int32)
    active = (down[:, 0:1] < pair_total).astype(jnp.int32)
    code_row = jnp.maximum(near, far) * (1 << FAR_SHIFT) + jnp.minimum(near, far)
    code_row = jnp.where(active_row > 0, code_row, -1)
    mark_row = jnp.where(near <= far, 256, 1) * active_row

    def across(values):
        return jnp.sum(values.astype(jnp.float32), axis=1, keepdims=True).astype(jnp.int32)

    code = across(jnp.where(down == along, code_row, 0))
    same = code == code_row
    tally = across(jnp.where(same, mark_row, 0))
    earlier = across(jnp.where(same, jnp.where(along < down, 1, 0), 0))
    first = jnp.where(earlier == 0, active, 0)
    first_row = jnp.sum(jnp.where(down == along, first, 0), axis=0, keepdims=True)
    place = across(jnp.where(code_row < code, first_row, 0))
    place = jnp.where(first > 0, place, -1)
    hit = place == along
    list_ref[0:1] = jnp.sum(jnp.where(hit, code, 0), axis=0, keepdims=True)
    list_ref[1:2] = jnp.sum(jnp.where(hit, tally, 0), axis=0, keepdims=True)
    list_ref[2:3] = jnp.sum(jnp.broadcast_to(first, shape), axis=0, keepdims=True)


def exchange_kernel(
    data_ref, type_ref, info_ref, send_ref, count_ref, pair_ref, total_ref,
    in_ref, all_ids_ref, list_ref,
    packed, ids, got, got_ids, send_sem, recv_sem, id_send, id_recv,
):
    homes, rows, width = in_ref.shape
    capacity = send_ref.shape[1]
    subs = all_ids_ref.shape[0]
    back_rows = ids.shape[1] // homes
    reps = lax.axis_size("rep")
    me = lax.axis_index("box") * reps + lax.axis_index("rep")
    sub = lax.axis_index("sub")
    barrier = pltpu.get_barrier_semaphore()
    unroll = homes <= 8

    def greet(step, _):
        peer = lax.rem(me + step, homes)
        pl.semaphore_signal(barrier, inc=1, device_id=box_rep(peer, reps), device_id_type=MESH)
        return 0

    def greet_sub(step, _):
        pl.semaphore_signal(barrier, inc=1, device_id={"sub": lax.rem(sub + step, subs)}, device_id_type=MESH)
        return 0

    lax.fori_loop(1, homes, greet, 0, unroll=unroll)
    lax.fori_loop(1, subs, greet_sub, 0, unroll=True)

    lane = lax.broadcasted_iota(jnp.int32, (1, width), 1)
    id_lane = lax.broadcasted_iota(jnp.int32, (1, ids.shape[1]), 1)

    def fill(home, row_ids):
        runs = jnp.zeros((1, width), jnp.int32)
        for column in range(capacity):
            tile = send_ref[0, column, 0, home]
            present = jnp.where(column < count_ref[0, 0, home], info_ref[0, 0, tile], 0)
            live = lane < present
            atoms = data_ref[0, tile]
            base = FIELDS * column
            packed[home, base : base + 3] = atoms[0:3]
            packed[home, base + 3 : base + 4] = jnp.where(live, atoms[3:4], 0.0)
            kinds = jnp.where(live, type_ref[0, pl.ds(tile, 1)], -1)
            packed[home, base + 4 : base + 5] = kinds.astype(jnp.float32)
            runs = jnp.where(lane == column, info_ref[0, 1, tile], runs)
            place = id_lane - (home * back_rows + 3 * column)
            row_ids = jnp.where((place >= 0) & (place < 3), 3 * tile + place, row_ids)
        base = FIELDS * capacity
        packed[home, base : base + 1] = runs.astype(jnp.float32)
        for row in range(base + 1, rows):
            packed[home, row : row + 1] = jnp.zeros((1, width), jnp.float32)
        return row_ids

    row_ids = lax.fori_loop(0, homes, fill, jnp.full(id_lane.shape, -1, jnp.int32), unroll=unroll)
    ids[...] = jnp.broadcast_to(row_ids.astype(jnp.float32), ids.shape)
    pl.semaphore_wait(barrier, homes - 1 + subs - 1)

    def to_home(step):
        peer = lax.rem(me + step, homes)
        return pltpu.make_async_remote_copy(
            src_ref=packed.at[peer],
            dst_ref=got.at[step],
            send_sem=send_sem.at[step],
            recv_sem=recv_sem.at[step],
            device_id=box_rep(peer, reps),
            device_id_type=MESH,
        )

    def to_sub(step):
        return pltpu.make_async_remote_copy(
            src_ref=ids,
            dst_ref=got_ids.at[step],
            send_sem=id_send.at[step],
            recv_sem=id_recv.at[step],
            device_id={"sub": lax.rem(sub + step, subs)},
            device_id_type=MESH,
        )

    def start(step, _):
        to_home(step).start()
        return 0

    def start_sub(step, _):
        to_sub(step).start()
        return 0

    lax.fori_loop(1, homes, start, 0, unroll=unroll)
    lax.fori_loop(1, subs, start_sub, 0, unroll=True)
    in_ref[me] = packed[me]
    all_ids_ref[sub] = ids[...]
    list_pairs(pair_ref, total_ref[0, 0], list_ref)

    def finish(step, _):
        to_home(step).wait()
        in_ref[lax.rem(me + homes - step, homes)] = got[step]
        return 0

    def finish_sub(step, _):
        to_sub(step).wait()
        all_ids_ref[lax.rem(sub + subs - step, subs)] = got_ids[step]
        return 0

    lax.fori_loop(1, homes, finish, 0, unroll=unroll)
    lax.fori_loop(1, subs, finish_sub, 0, unroll=True)


def exchange(data, kinds, info, chosen, counts, pairs, totals, subs):
    homes, capacity = chosen.shape[2:]
    width = data.shape[3]
    block = (homes, padded(FIELDS * capacity + 1), width)
    id_block = (8, homes * padded(3 * capacity))
    return pl.pallas_call(
        exchange_kernel,
        out_shape=(
            jax.ShapeDtypeStruct(block, jnp.float32),
            jax.ShapeDtypeStruct((subs,) + id_block, jnp.float32),
            jax.ShapeDtypeStruct((3, pairs.shape[2]), jnp.int32),
        ),
        in_specs=[spec(VMEM), spec(VMEM), spec(SMEM), spec(SMEM), spec(SMEM), spec(VMEM), spec(SMEM)],
        out_specs=(spec(VMEM),) * 3,
        scratch_shapes=[
            VMEM(block, jnp.float32),
            VMEM(id_block, jnp.float32),
            VMEM(block, jnp.float32),
            VMEM((subs,) + id_block, jnp.float32),
            pltpu.SemaphoreType.DMA((homes,)),
            pltpu.SemaphoreType.DMA((homes,)),
            pltpu.SemaphoreType.DMA((subs,)),
            pltpu.SemaphoreType.DMA((subs,)),
        ],
        compiler_params=pltpu.CompilerParams(collective_id=0, has_side_effects=True),
    )(
        data,
        kinds,
        jnp.transpose(info, (0, 2, 1)),
        jnp.transpose(chosen, (0, 3, 1, 2)),
        counts,
        jnp.transpose(pairs, (0, 1, 3, 2)),
        totals,
    )


def force_kernel(list_ref, rep_ref, dis_ref, in_ref, out_ref, kind_ref, rec_ref, far_ref, back_ref, slot_ref):
    slots, width = kind_ref.shape
    homes = out_ref.shape[0]
    capacity = slots // homes
    reach_sq = CUTOFF_SQ + SOFTENING
    reach = reach_sq**0.5
    scale = reach_sq * reach / (CUTOFF_SQ * CUTOFF_SQ)
    diag = lax.broadcasted_iota(jnp.int32, (width, width), 0) == lax.broadcasted_iota(jnp.int32, (width, width), 1)
    lane = lax.broadcasted_iota(jnp.int32, (1, width), 1)
    atom_row = lane.astype(jnp.float32) + 0.5

    def unpack(home, _):
        runs = in_ref[home, FIELDS * capacity : FIELDS * capacity + 1]
        for column in range(capacity):
            slot = home * capacity + column
            base = FIELDS * column
            rec_ref[slot, 0:3] = in_ref[home, base : base + 3] * (1.0 / reach)
            rec_ref[slot, 3:4] = in_ref[home, base + 3 : base + 4]
            kind_ref[pl.ds(slot, 1)] = in_ref[home, base + 4 : base + 5]
            run = jnp.sum(jnp.where(lane == column, runs, 0.0), axis=1, keepdims=True)
            rec_ref[slot, 6:7] = jnp.broadcast_to(1.0 / run, (1, width))
            slot_ref[slot] = jnp.zeros(slot_ref.shape[1:], jnp.float32)
        return 0

    lax.fori_loop(0, homes, unpack, 0, unroll=homes <= 8)
    slot_ref[slots] = jnp.zeros(slot_ref.shape[1:], jnp.float32)
    kinds = kind_ref[...]
    repulsion = jnp.zeros(kinds.shape, jnp.float32)
    dispersion = jnp.zeros(kinds.shape, jnp.float32)
    for kind in range(rep_ref.shape[0]):
        match = kinds == float(kind)
        repulsion = jnp.where(match, rep_ref[kind], repulsion)
        dispersion = jnp.where(match, dis_ref[kind], dispersion)
    rec_ref[:, 4] = repulsion
    rec_ref[:, 5] = dispersion
    back_ref[...] = jnp.zeros(back_ref.shape, jnp.float32)

    def close_group(far):
        for axis in range(3):
            folded = jnp.sum(jnp.transpose(back_ref[axis]).reshape(width // 8, 8, width), axis=0)
            slot_ref[far, axis] = slot_ref[far, axis] - folded

    def change_group(closed, far):
        rows = rec_ref[far]
        for field in range(6):
            far_ref[field] = jnp.transpose(jnp.broadcast_to(rows[field : field + 1], (width, width)))
        close_group(closed)
        back_ref[...] = jnp.zeros(back_ref.shape, jnp.float32)

    def tile_pair(near, near_scale, far_scale, own, both):
        rows = rec_ref[near]
        x, y, z = rows[0:1], rows[1:2], rows[2:3]
        charge = rows[3:4] * (far_scale * (COULOMB * scale / reach))
        rep = rows[4:5] * (far_scale * (12.0 * scale / reach_sq**6))
        dis = rows[5:6] * (far_scale * (6.0 * scale / reach_sq**3))
        if own:
            per_run = rows[6:7]
            mol = jnp.floor(atom_row * per_run)
        sums = [jnp.zeros((8, width), jnp.float32) for _ in range(3)]
        for start in range(0, width, CHUNK):
            at = slice(start, start + CHUNK)
            dx = x - far_ref[0, at]
            dy = y - far_ref[1, at]
            dz = z - far_ref[2, at]
            soft = dx * dx + dy * dy + (dz * dz + SOFTENING / reach_sq)
            root = lax.rsqrt(soft)
            inverse = root * root
            cube = inverse * inverse * inverse
            window = jnp.maximum(1.0 - soft, 0.0)
            first = (rep * far_ref[4, at]) * cube * (inverse - 2.0 / 3.0)
            second = (dis * far_ref[5, at]) * (inverse - 1.0 / 3.0)
            third = (charge * far_ref[3, at]) * root * (inverse + 3.0)
            weight = ((first - second) * cube + third) * window
            if own:
                atoms = lax.broadcasted_iota(jnp.int32, (CHUNK, width), 0).astype(jnp.float32) + (start + 0.5)
                weight = jnp.where(mol == jnp.floor(atoms * per_run), 0.0, weight)
            for axis, step in enumerate((dx, dy, dz)):
                term = weight * step
                sums[axis] = sums[axis] + jnp.sum(term.reshape(CHUNK // 8, 8, width), axis=0)
                if both:
                    back_ref[axis, at] = back_ref[axis, at] + term
        for axis in range(3):
            slot_ref[near, axis] = slot_ref[near, axis] + sums[axis] * near_scale

    used = list_ref[2, 0]

    def visit(index, open_slot):
        code = list_ref[0, index]
        tally = list_ref[1, index]
        far = code >> FAR_SHIFT
        near = code & ((1 << FAR_SHIFT) - 1)
        forward = (tally >> 8).astype(jnp.float32)
        backward_count = tally & 255
        backward = backward_count.astype(jnp.float32)

        @pl.when(far != open_slot)
        def _():
            change_group(open_slot, far)

        both = backward_count > 0

        @pl.when(both)
        def _():
            ratio = jnp.full((8, width), forward, jnp.float32) / jnp.full((8, width), backward, jnp.float32)
            tile_pair(near, ratio, backward, False, True)

        @pl.when(jnp.logical_not(both))
        def _():
            @pl.when(near == far)
            def _():
                tile_pair(near, forward, 1.0, True, False)

            @pl.when(near != far)
            def _():
                tile_pair(near, forward, 1.0, False, False)

        return far

    close_group(lax.fori_loop(0, used, visit, jnp.int32(slots)))

    def finish(home, _):
        for column in range(capacity):
            for axis in range(3):
                row = 3 * column + axis
                out_ref[home, row : row + 1] = jnp.sum(slot_ref[home * capacity + column, axis], axis=0, keepdims=True)
        for row in range(3 * capacity, out_ref.shape[1]):
            out_ref[home, row : row + 1] = jnp.zeros((1, width), jnp.float32)
        return 0

    lax.fori_loop(0, homes, finish, 0, unroll=homes <= 8)


def slot_forces(listed, repulsion, dispersion, incoming, capacity):
    homes, _, width = incoming.shape
    slots = homes * capacity
    return pl.pallas_call(
        force_kernel,
        out_shape=jax.ShapeDtypeStruct((homes, padded(3 * capacity), width), jnp.float32),
        in_specs=[spec(SMEM), spec(SMEM), spec(SMEM), spec(VMEM)],
        out_specs=spec(VMEM),
        scratch_shapes=[
            VMEM((slots, width), jnp.float32),
            VMEM((slots, 8, width), jnp.float32),
            VMEM((6, width, width), jnp.float32),
            VMEM((3, width, width), jnp.float32),
            VMEM((slots + 1, 3, 8, width), jnp.float32),
        ],
    )(listed, repulsion, dispersion, incoming)


def return_kernel(force_ref, ids_ref, out_ref, got, send_sem, recv_sem):
    homes, rows, width = force_ref.shape
    subs = ids_ref.shape[0]
    reps = lax.axis_size("rep")
    me = lax.axis_index("box") * reps + lax.axis_index("rep")
    sub = lax.axis_index("sub")
    total = subs * homes
    mine = sub * homes + me
    barrier = pltpu.get_barrier_semaphore()

    def place(step):
        peer = lax.rem(mine + step, total)
        home = lax.rem(peer, homes)
        return home, {"sub": peer // homes, "box": home // reps, "rep": lax.rem(home, reps)}

    def greet(step, _):
        pl.semaphore_signal(barrier, inc=1, device_id=place(step)[1], device_id_type=MESH)
        return 0

    lax.fori_loop(1, total, greet, 0, unroll=total <= 16)
    pl.semaphore_wait(barrier, total - 1)

    def copy(step):
        home, device = place(step)
        return pltpu.make_async_remote_copy(
            src_ref=force_ref.at[home],
            dst_ref=got.at[mine],
            send_sem=send_sem.at[step],
            recv_sem=recv_sem.at[step],
            device_id=device,
            device_id_type=MESH,
        )

    def start(step, _):
        copy(step).start()
        return 0

    def finish(step, _):
        copy(step).wait()
        return 0

    lax.fori_loop(1, total, start, 0, unroll=total <= 16)
    got[mine] = force_ref[me]
    lax.fori_loop(1, total, finish, 0, unroll=total <= 16)
    tiles = out_ref.shape[0]
    held = 3 * tiles
    wanted = lax.broadcasted_iota(jnp.int32, (held, homes * rows), 0) + sub * held
    wanted = wanted.astype(jnp.float32)
    result = jnp.zeros((held, width), jnp.float32)
    for plane in range(subs):
        pick = (ids_ref[plane, 0:1] == wanted).astype(jnp.float32)
        block = got[plane * homes : (plane + 1) * homes].reshape(homes * rows, width)
        result = result + jnp.dot(
            pick, block, precision=lax.Precision.HIGHEST, preferred_element_type=jnp.float32
        )
    for row in range(held):
        out_ref[row // 3, row % 3] = result[row : row + 1]


def send_back(forces, ids, held):
    homes, rows, width = forces.shape
    subs = ids.shape[0]
    return pl.pallas_call(
        return_kernel,
        out_shape=jax.ShapeDtypeStruct((held, 3, 1, width), jnp.float32),
        in_specs=[spec(VMEM), spec(VMEM)],
        out_specs=spec(VMEM),
        scratch_shapes=[
            VMEM((subs * homes, rows, width), jnp.float32),
            pltpu.SemaphoreType.DMA((subs * homes,)),
            pltpu.SemaphoreType.DMA((subs * homes,)),
        ],
        compiler_params=pltpu.CompilerParams(collective_id=1, has_side_effects=True),
    )(forces, ids)


def per_device(
    atom_data, atom_type, tile_info, lj_repulsion, lj_dispersion, send_tiles, send_count, pair_slots, pair_count
):
    subs = lax.axis_size("sub")
    incoming, ids, listed = exchange(
        atom_data, atom_type, tile_info, send_tiles, send_count, pair_slots, pair_count, subs
    )
    forces = slot_forces(listed, lj_repulsion, lj_dispersion, incoming, send_tiles.shape[3])
    result = send_back(forces, ids, atom_data.shape[1] // subs)
    return jnp.transpose(result, (2, 0, 1, 3))


def solution(mesh):
    placed = (
        P(("groups", "box", "rep"), None, None, None),
        P(("groups", "box", "rep"), None, None),
        P(("groups", "box", "rep"), None, None),
        P(),
        P(),
        P(("groups", "box", "rep"), "sub", None, None),
        P(("groups", "box", "rep"), "sub", None),
        P(("groups", "box", "rep"), "sub", None, None),
        P(("groups", "box", "rep"), "sub"),
    )
    return jax.shard_map(
        per_device,
        mesh=mesh,
        in_specs=placed,
        out_specs=P(("groups", "box", "rep"), "sub", None, None),
        check_vma=False,
    )
```

```python
import functools

import jax
import jax.numpy as jnp
from jax import lax
from jax.experimental import pallas as pl
from jax.experimental.pallas import tpu as pltpu
from jax.sharding import PartitionSpec as P

COULOMB = 332.0636
SOFTENING = 9.0
CUTOFF_SQ = 144.0
MESH = pl.DeviceIdType.MESH
FIELDS = 5
CHUNK = 16
FAR_SHIFT = 12
VMEM = pltpu.VMEM
SMEM = pltpu.SMEM


def spec(space):
    return pl.BlockSpec(memory_space=space)


def padded(rows):
    return -(-rows // 8) * 8


def box_rep(home, reps):
    return {"box": home // reps, "rep": lax.rem(home, reps)}


def list_pairs(pair_ref, pair_total, list_ref):
    pair_max = list_ref.shape[1]
    shape = (pair_max, pair_max)
    down = lax.broadcasted_iota(jnp.int32, shape, 0)
    along = lax.broadcasted_iota(jnp.int32, shape, 1)
    near, far = pair_ref[0, 0, 0:1], pair_ref[0, 0, 1:2]
    active_row = (along[0:1] < pair_total).astype(jnp.int32)
    active = (down[:, 0:1] < pair_total).astype(jnp.int32)
    code_row = jnp.maximum(near, far) * (1 << FAR_SHIFT) + jnp.minimum(near, far)
    code_row = jnp.where(active_row > 0, code_row, -1)
    mark_row = jnp.where(near <= far, 256, 1) * active_row

    def across(values):
        return jnp.sum(values.astype(jnp.float32), axis=1, keepdims=True).astype(jnp.int32)

    code = across(jnp.where(down == along, code_row, 0))
    same = code == code_row
    tally = across(jnp.where(same, mark_row, 0))
    earlier = across(jnp.where(same, jnp.where(along < down, 1, 0), 0))
    first = jnp.where(earlier == 0, active, 0)
    first_row = jnp.sum(jnp.where(down == along, first, 0), axis=0, keepdims=True)
    place = across(jnp.where(code_row < code, first_row, 0))
    place = jnp.where(first > 0, place, -1)
    hit = place == along
    list_ref[0:1] = jnp.sum(jnp.where(hit, code, 0), axis=0, keepdims=True)
    list_ref[1:2] = jnp.sum(jnp.where(hit, tally, 0), axis=0, keepdims=True)
    list_ref[2:3] = jnp.sum(jnp.broadcast_to(first, shape), axis=0, keepdims=True)


def exchange_kernel(
    data_ref, type_ref, info_ref, send_ref, count_ref, pair_ref, total_ref,
    in_ref, all_ids_ref, list_ref,
    packed, ids, got, got_ids, send_sem, recv_sem, id_send, id_recv,
):
    homes, rows, width = in_ref.shape
    capacity = send_ref.shape[1]
    subs = all_ids_ref.shape[0]
    back_rows = ids.shape[1] // homes
    reps = lax.axis_size("rep")
    me = lax.axis_index("box") * reps + lax.axis_index("rep")
    sub = lax.axis_index("sub")
    barrier = pltpu.get_barrier_semaphore()
    unroll = homes <= 8

    def greet(step, _):
        peer = lax.rem(me + step, homes)
        pl.semaphore_signal(barrier, inc=1, device_id=box_rep(peer, reps), device_id_type=MESH)
        return 0

    def greet_sub(step, _):
        pl.semaphore_signal(barrier, inc=1, device_id={"sub": lax.rem(sub + step, subs)}, device_id_type=MESH)
        return 0

    lax.fori_loop(1, homes, greet, 0, unroll=unroll)
    lax.fori_loop(1, subs, greet_sub, 0, unroll=True)

    lane = lax.broadcasted_iota(jnp.int32, (1, width), 1)
    id_lane = lax.broadcasted_iota(jnp.int32, (1, ids.shape[1]), 1)

    def fill(home, row_ids):
        runs = jnp.zeros((1, width), jnp.int32)
        for column in range(capacity):
            tile = send_ref[0, column, 0, home]
            present = jnp.where(column < count_ref[0, 0, home], info_ref[0, 0, tile], 0)
            live = lane < present
            atoms = data_ref[0, tile]
            base = FIELDS * column
            packed[home, base : base + 3] = atoms[0:3]
            packed[home, base + 3 : base + 4] = jnp.where(live, atoms[3:4], 0.0)
            kinds = jnp.where(live, type_ref[0, pl.ds(tile, 1)], -1)
            packed[home, base + 4 : base + 5] = kinds.astype(jnp.float32)
            runs = jnp.where(lane == column, info_ref[0, 1, tile], runs)
            place = id_lane - (home * back_rows + 3 * column)
            row_ids = jnp.where((place >= 0) & (place < 3), 3 * tile + place, row_ids)
        base = FIELDS * capacity
        packed[home, base : base + 1] = runs.astype(jnp.float32)
        for row in range(base + 1, rows):
            packed[home, row : row + 1] = jnp.zeros((1, width), jnp.float32)
        return row_ids

    row_ids = lax.fori_loop(0, homes, fill, jnp.full(id_lane.shape, -1, jnp.int32), unroll=unroll)
    ids[...] = jnp.broadcast_to(row_ids.astype(jnp.float32), ids.shape)
    pl.semaphore_wait(barrier, homes - 1 + subs - 1)

    def to_home(step):
        peer = lax.rem(me + step, homes)
        return pltpu.make_async_remote_copy(
            src_ref=packed.at[peer],
            dst_ref=got.at[step],
            send_sem=send_sem.at[step],
            recv_sem=recv_sem.at[step],
            device_id=box_rep(peer, reps),
            device_id_type=MESH,
        )

    def to_sub(step):
        return pltpu.make_async_remote_copy(
            src_ref=ids,
            dst_ref=got_ids.at[step],
            send_sem=id_send.at[step],
            recv_sem=id_recv.at[step],
            device_id={"sub": lax.rem(sub + step, subs)},
            device_id_type=MESH,
        )

    def start(step, _):
        to_home(step).start()
        return 0

    def start_sub(step, _):
        to_sub(step).start()
        return 0

    lax.fori_loop(1, homes, start, 0, unroll=unroll)
    lax.fori_loop(1, subs, start_sub, 0, unroll=True)
    in_ref[me] = packed[me]
    all_ids_ref[sub] = ids[...]
    list_pairs(pair_ref, total_ref[0, 0], list_ref)

    def finish(step, _):
        to_home(step).wait()
        in_ref[lax.rem(me + homes - step, homes)] = got[step]
        return 0

    def finish_sub(step, _):
        to_sub(step).wait()
        all_ids_ref[lax.rem(sub + subs - step, subs)] = got_ids[step]
        return 0

    lax.fori_loop(1, homes, finish, 0, unroll=unroll)
    lax.fori_loop(1, subs, finish_sub, 0, unroll=True)


def exchange(data, kinds, info, chosen, counts, pairs, totals, subs):
    homes, capacity = chosen.shape[2:]
    width = data.shape[3]
    block = (homes, padded(FIELDS * capacity + 1), width)
    id_block = (8, homes * padded(3 * capacity))
    return pl.pallas_call(
        exchange_kernel,
        out_shape=(
            jax.ShapeDtypeStruct(block, jnp.float32),
            jax.ShapeDtypeStruct((subs,) + id_block, jnp.float32),
            jax.ShapeDtypeStruct((3, pairs.shape[2]), jnp.int32),
        ),
        in_specs=[spec(VMEM), spec(VMEM), spec(SMEM), spec(SMEM), spec(SMEM), spec(VMEM), spec(SMEM)],
        out_specs=(spec(VMEM),) * 3,
        scratch_shapes=[
            VMEM(block, jnp.float32),
            VMEM(id_block, jnp.float32),
            VMEM(block, jnp.float32),
            VMEM((subs,) + id_block, jnp.float32),
            pltpu.SemaphoreType.DMA((homes,)),
            pltpu.SemaphoreType.DMA((homes,)),
            pltpu.SemaphoreType.DMA((subs,)),
            pltpu.SemaphoreType.DMA((subs,)),
        ],
        compiler_params=pltpu.CompilerParams(collective_id=0, has_side_effects=True),
    )(
        data,
        kinds,
        jnp.transpose(info, (0, 2, 1)),
        jnp.transpose(chosen, (0, 3, 1, 2)),
        counts,
        jnp.transpose(pairs, (0, 1, 3, 2)),
        totals,
    )


def force_kernel(list_ref, rep_ref, dis_ref, in_ref, out_ref, kind_ref, rec_ref, far_ref, back_ref, slot_ref):
    slots, width = kind_ref.shape
    homes = out_ref.shape[0]
    capacity = slots // homes
    reach_sq = CUTOFF_SQ + SOFTENING
    reach = reach_sq**0.5
    scale = reach_sq * reach / (CUTOFF_SQ * CUTOFF_SQ)
    diag = lax.broadcasted_iota(jnp.int32, (width, width), 0) == lax.broadcasted_iota(jnp.int32, (width, width), 1)
    lane = lax.broadcasted_iota(jnp.int32, (1, width), 1)
    atom_row = lane.astype(jnp.float32) + 0.5

    def unpack(home, _):
        runs = in_ref[home, FIELDS * capacity : FIELDS * capacity + 1]
        for column in range(capacity):
            slot = home * capacity + column
            base = FIELDS * column
            rec_ref[slot, 0:3] = in_ref[home, base : base + 3] * (1.0 / reach)
            rec_ref[slot, 3:4] = in_ref[home, base + 3 : base + 4]
            kind_ref[pl.ds(slot, 1)] = in_ref[home, base + 4 : base + 5]
            run = jnp.sum(jnp.where(lane == column, runs, 0.0), axis=1, keepdims=True)
            rec_ref[slot, 6:7] = jnp.broadcast_to(1.0 / run, (1, width))
            slot_ref[slot] = jnp.zeros(slot_ref.shape[1:], jnp.float32)
        return 0

    lax.fori_loop(0, homes, unpack, 0, unroll=homes <= 8)
    slot_ref[slots] = jnp.zeros(slot_ref.shape[1:], jnp.float32)
    kinds = kind_ref[...]
    repulsion = jnp.zeros(kinds.shape, jnp.float32)
    dispersion = jnp.zeros(kinds.shape, jnp.float32)
    for kind in range(rep_ref.shape[0]):
        match = kinds == float(kind)
        repulsion = jnp.where(match, rep_ref[kind], repulsion)
        dispersion = jnp.where(match, dis_ref[kind], dispersion)
    rec_ref[:, 4] = repulsion
    rec_ref[:, 5] = dispersion
    back_ref[...] = jnp.zeros(back_ref.shape, jnp.float32)

    def close_group(far):
        for axis in range(3):
            folded = jnp.sum(jnp.transpose(back_ref[axis]).reshape(width // 8, 8, width), axis=0)
            slot_ref[far, axis] = slot_ref[far, axis] - folded

    def change_group(closed, far):
        rows = rec_ref[far]
        for field in range(6):
            far_ref[field] = jnp.transpose(jnp.broadcast_to(rows[field : field + 1], (width, width)))
        close_group(closed)
        back_ref[...] = jnp.zeros(back_ref.shape, jnp.float32)

    def tile_pair(near, near_scale, far_scale, own, both):
        rows = rec_ref[near]
        x, y, z = rows[0:1], rows[1:2], rows[2:3]
        charge = rows[3:4] * (far_scale * (COULOMB * scale / reach))
        rep = rows[4:5] * (far_scale * (12.0 * scale / reach_sq**6))
        dis = rows[5:6] * (far_scale * (6.0 * scale / reach_sq**3))
        if own:
            per_run = rows[6:7]
            mol = jnp.floor(atom_row * per_run)
        sums = [jnp.zeros((8, width), jnp.float32) for _ in range(3)]
        for start in range(0, width, CHUNK):
            at = slice(start, start + CHUNK)
            dx = x - far_ref[0, at]
            dy = y - far_ref[1, at]
            dz = z - far_ref[2, at]
            soft = dx * dx + dy * dy + (dz * dz + SOFTENING / reach_sq)
            root = lax.rsqrt(soft)
            inverse = root * root
            cube = inverse * inverse * inverse
            window = jnp.maximum(1.0 - soft, 0.0)
            first = (rep * far_ref[4, at]) * cube * (inverse - 2.0 / 3.0)
            second = (dis * far_ref[5, at]) * (inverse - 1.0 / 3.0)
            third = (charge * far_ref[3, at]) * root * (inverse + 3.0)
            weight = ((first - second) * cube + third) * window
            if own:
                atoms = lax.broadcasted_iota(jnp.int32, (CHUNK, width), 0).astype(jnp.float32) + (start + 0.5)
                weight = jnp.where(mol == jnp.floor(atoms * per_run), 0.0, weight)
            for axis, step in enumerate((dx, dy, dz)):
                term = weight * step
                sums[axis] = sums[axis] + jnp.sum(term.reshape(CHUNK // 8, 8, width), axis=0)
                if both:
                    back_ref[axis, at] = back_ref[axis, at] + term
        for axis in range(3):
            slot_ref[near, axis] = slot_ref[near, axis] + sums[axis] * near_scale

    used = list_ref[2, 0]

    def visit(index, open_slot):
        code = list_ref[0, index]
        tally = list_ref[1, index]
        far = code >> FAR_SHIFT
        near = code & ((1 << FAR_SHIFT) - 1)
        forward = (tally >> 8).astype(jnp.float32)
        backward_count = tally & 255
        backward = backward_count.astype(jnp.float32)

        @pl.when(far != open_slot)
        def _():
            change_group(open_slot, far)

        both = backward_count > 0

        @pl.when(both)
        def _():
            ratio = jnp.full((8, width), forward, jnp.float32) / jnp.full((8, width), backward, jnp.float32)
            tile_pair(near, ratio, backward, False, True)

        @pl.when(jnp.logical_not(both))
        def _():
            @pl.when(near == far)
            def _():
                tile_pair(near, forward, 1.0, True, False)

            @pl.when(near != far)
            def _():
                tile_pair(near, forward, 1.0, False, False)

        return far

    close_group(lax.fori_loop(0, used, visit, jnp.int32(slots)))

    def finish(home, _):
        for column in range(capacity):
            for axis in range(3):
                row = 3 * column + axis
                out_ref[home, row : row + 1] = jnp.sum(slot_ref[home * capacity + column, axis], axis=0, keepdims=True)
        for row in range(3 * capacity, out_ref.shape[1]):
            out_ref[home, row : row + 1] = jnp.zeros((1, width), jnp.float32)
        return 0

    lax.fori_loop(0, homes, finish, 0, unroll=homes <= 8)


def slot_forces(listed, repulsion, dispersion, incoming, capacity):
    homes, _, width = incoming.shape
    slots = homes * capacity
    return pl.pallas_call(
        force_kernel,
        out_shape=jax.ShapeDtypeStruct((homes, padded(3 * capacity), width), jnp.float32),
        in_specs=[spec(SMEM), spec(SMEM), spec(SMEM), spec(VMEM)],
        out_specs=spec(VMEM),
        scratch_shapes=[
            VMEM((slots, width), jnp.float32),
            VMEM((slots, 8, width), jnp.float32),
            VMEM((6, width, width), jnp.float32),
            VMEM((3, width, width), jnp.float32),
            VMEM((slots + 1, 3, 8, width), jnp.float32),
        ],
    )(listed, repulsion, dispersion, incoming)


def return_kernel(used, force_ref, ids_ref, out_ref, got, send_sem, recv_sem):
    homes, rows, width = force_ref.shape
    subs = ids_ref.shape[0]
    reps = lax.axis_size("rep")
    me = lax.axis_index("box") * reps + lax.axis_index("rep")
    sub = lax.axis_index("sub")
    total = subs * homes
    mine = sub * homes + me
    got[...] = jnp.zeros(got.shape, jnp.float32)
    barrier = pltpu.get_barrier_semaphore()

    def place(step):
        peer = lax.rem(mine + step, total)
        home = lax.rem(peer, homes)
        return home, {"sub": peer // homes, "box": home // reps, "rep": lax.rem(home, reps)}

    def greet(step, _):
        pl.semaphore_signal(barrier, inc=1, device_id=place(step)[1], device_id_type=MESH)
        return 0

    lax.fori_loop(1, total, greet, 0, unroll=total <= 16)
    pl.semaphore_wait(barrier, total - 1)

    def copy(step):
        home, device = place(step)
        return pltpu.make_async_remote_copy(
            src_ref=force_ref.at[home, pl.ds(0, used)],
            dst_ref=got.at[mine, pl.ds(0, used)],
            send_sem=send_sem.at[step],
            recv_sem=recv_sem.at[step],
            device_id=device,
            device_id_type=MESH,
        )

    def start(step, _):
        copy(step).start()
        return 0

    def finish(step, _):
        copy(step).wait()
        return 0

    lax.fori_loop(1, total, start, 0, unroll=total <= 16)
    got[mine] = force_ref[me]
    lax.fori_loop(1, total, finish, 0, unroll=total <= 16)
    tiles = out_ref.shape[0]
    held = 3 * tiles
    wanted = lax.broadcasted_iota(jnp.int32, (held, homes * rows), 0) + sub * held
    wanted = wanted.astype(jnp.float32)
    result = jnp.zeros((held, width), jnp.float32)
    for plane in range(subs):
        pick = (ids_ref[plane, 0:1] == wanted).astype(jnp.float32)
        block = got[plane * homes : (plane + 1) * homes].reshape(homes * rows, width)
        result = result + jnp.dot(
            pick, block, precision=lax.Precision.HIGHEST, preferred_element_type=jnp.float32
        )
    for row in range(held):
        out_ref[row // 3, row % 3] = result[row : row + 1]


def send_back(forces, ids, held, used):
    homes, rows, width = forces.shape
    subs = ids.shape[0]
    return pl.pallas_call(
        functools.partial(return_kernel, used),
        out_shape=jax.ShapeDtypeStruct((held, 3, 1, width), jnp.float32),
        in_specs=[spec(VMEM), spec(VMEM)],
        out_specs=spec(VMEM),
        scratch_shapes=[
            VMEM((subs * homes, rows, width), jnp.float32),
            pltpu.SemaphoreType.DMA((subs * homes,)),
            pltpu.SemaphoreType.DMA((subs * homes,)),
        ],
        compiler_params=pltpu.CompilerParams(collective_id=1, has_side_effects=True),
    )(forces, ids)


def per_device(
    atom_data, atom_type, tile_info, lj_repulsion, lj_dispersion, send_tiles, send_count, pair_slots, pair_count
):
    subs = lax.axis_size("sub")
    incoming, ids, listed = exchange(
        atom_data, atom_type, tile_info, send_tiles, send_count, pair_slots, pair_count, subs
    )
    forces = slot_forces(listed, lj_repulsion, lj_dispersion, incoming, send_tiles.shape[3])
    result = send_back(forces, ids, atom_data.shape[1] // subs, 3 * send_tiles.shape[3])
    return jnp.transpose(result, (2, 0, 1, 3))


def solution(mesh):
    placed = (
        P(("groups", "box", "rep"), None, None, None),
        P(("groups", "box", "rep"), None, None),
        P(("groups", "box", "rep"), None, None),
        P(),
        P(),
        P(("groups", "box", "rep"), "sub", None, None),
        P(("groups", "box", "rep"), "sub", None),
        P(("groups", "box", "rep"), "sub", None, None),
        P(("groups", "box", "rep"), "sub"),
    )
    return jax.shard_map(
        per_device,
        mesh=mesh,
        in_specs=placed,
        out_specs=P(("groups", "box", "rep"), "sub", None, None),
        check_vma=False,
    )
```

```python
import functools

import jax
import jax.numpy as jnp
from jax import lax
from jax.experimental import pallas as pl
from jax.experimental.pallas import tpu as pltpu
from jax.sharding import PartitionSpec as P

COULOMB = 332.0636
SOFTENING = 9.0
CUTOFF_SQ = 144.0
MESH = pl.DeviceIdType.MESH
FIELDS = 5
CHUNK = 16
FAR_SHIFT = 12
VMEM = pltpu.VMEM
SMEM = pltpu.SMEM


def spec(space):
    return pl.BlockSpec(memory_space=space)


def padded(rows):
    return -(-rows // 8) * 8


def box_rep(home, reps):
    return {"box": home // reps, "rep": lax.rem(home, reps)}


def list_pairs(pair_ref, pair_total, list_ref):
    pair_max = list_ref.shape[1]
    shape = (pair_max, pair_max)
    down = lax.broadcasted_iota(jnp.int32, shape, 0)
    along = lax.broadcasted_iota(jnp.int32, shape, 1)
    near, far = pair_ref[0, 0, 0:1], pair_ref[0, 0, 1:2]
    active_row = (along[0:1] < pair_total).astype(jnp.int32)
    active = (down[:, 0:1] < pair_total).astype(jnp.int32)
    code_row = jnp.maximum(near, far) * (1 << FAR_SHIFT) + jnp.minimum(near, far)
    code_row = jnp.where(active_row > 0, code_row, -1)
    mark_row = jnp.where(near <= far, 256, 1) * active_row

    def across(values):
        return jnp.sum(values.astype(jnp.float32), axis=1, keepdims=True).astype(jnp.int32)

    code = across(jnp.where(down == along, code_row, 0))
    same = code == code_row
    tally = across(jnp.where(same, mark_row, 0))
    earlier = across(jnp.where(same, jnp.where(along < down, 1, 0), 0))
    first = jnp.where(earlier == 0, active, 0)
    first_row = jnp.sum(jnp.where(down == along, first, 0), axis=0, keepdims=True)
    place = across(jnp.where(code_row < code, first_row, 0))
    place = jnp.where(first > 0, place, -1)
    hit = place == along
    list_ref[0:1] = jnp.sum(jnp.where(hit, code, 0), axis=0, keepdims=True)
    list_ref[1:2] = jnp.sum(jnp.where(hit, tally, 0), axis=0, keepdims=True)
    list_ref[2:3] = jnp.sum(jnp.broadcast_to(first, shape), axis=0, keepdims=True)


def exchange_kernel(
    data_ref, type_ref, info_ref, send_ref, count_ref, pair_ref, total_ref,
    in_ref, all_ids_ref, list_ref,
    packed, ids, got, got_ids, send_sem, recv_sem, id_send, id_recv,
):
    homes, rows, width = in_ref.shape
    capacity = send_ref.shape[1]
    subs = all_ids_ref.shape[0]
    back_rows = ids.shape[1] // homes
    reps = lax.axis_size("rep")
    me = lax.axis_index("box") * reps + lax.axis_index("rep")
    sub = lax.axis_index("sub")
    barrier = pltpu.get_barrier_semaphore()
    unroll = homes <= 8

    def greet(step, _):
        peer = lax.rem(me + step, homes)
        pl.semaphore_signal(barrier, inc=1, device_id=box_rep(peer, reps), device_id_type=MESH)
        return 0

    def greet_sub(step, _):
        pl.semaphore_signal(barrier, inc=1, device_id={"sub": lax.rem(sub + step, subs)}, device_id_type=MESH)
        return 0

    lax.fori_loop(1, homes, greet, 0, unroll=unroll)
    lax.fori_loop(1, subs, greet_sub, 0, unroll=True)

    lane = lax.broadcasted_iota(jnp.int32, (1, width), 1)
    id_lane = lax.broadcasted_iota(jnp.int32, (1, ids.shape[1]), 1)

    def fill(home, row_ids):
        runs = jnp.zeros((1, width), jnp.int32)
        for column in range(capacity):
            tile = send_ref[0, column, 0, home]
            present = jnp.where(column < count_ref[0, 0, home], info_ref[0, 0, tile], 0)
            live = lane < present
            atoms = data_ref[0, tile]
            base = FIELDS * column
            packed[home, base : base + 3] = atoms[0:3]
            packed[home, base + 3 : base + 4] = jnp.where(live, atoms[3:4], 0.0)
            kinds = jnp.where(live, type_ref[0, pl.ds(tile, 1)], -1)
            packed[home, base + 4 : base + 5] = kinds.astype(jnp.float32)
            runs = jnp.where(lane == column, info_ref[0, 1, tile], runs)
            place = id_lane - (home * back_rows + 3 * column)
            row_ids = jnp.where((place >= 0) & (place < 3), 3 * tile + place, row_ids)
        base = FIELDS * capacity
        packed[home, base : base + 1] = runs.astype(jnp.float32)
        for row in range(base + 1, rows):
            packed[home, row : row + 1] = jnp.zeros((1, width), jnp.float32)
        return row_ids

    row_ids = lax.fori_loop(0, homes, fill, jnp.full(id_lane.shape, -1, jnp.int32), unroll=unroll)
    ids[...] = jnp.broadcast_to(row_ids.astype(jnp.float32), ids.shape)
    pl.semaphore_wait(barrier, homes - 1 + subs - 1)

    def to_home(step):
        peer = lax.rem(me + step, homes)
        return pltpu.make_async_remote_copy(
            src_ref=packed.at[peer],
            dst_ref=got.at[step],
            send_sem=send_sem.at[step],
            recv_sem=recv_sem.at[step],
            device_id=box_rep(peer, reps),
            device_id_type=MESH,
        )

    def to_sub(step):
        return pltpu.make_async_remote_copy(
            src_ref=ids,
            dst_ref=got_ids.at[step],
            send_sem=id_send.at[step],
            recv_sem=id_recv.at[step],
            device_id={"sub": lax.rem(sub + step, subs)},
            device_id_type=MESH,
        )

    def start(step, _):
        to_home(1 + lax.rem(step + homes // 2 - 2, homes - 1)).start()
        return 0

    def start_sub(step, _):
        to_sub(step).start()
        return 0

    lax.fori_loop(1, homes, start, 0, unroll=unroll)
    lax.fori_loop(1, subs, start_sub, 0, unroll=True)
    in_ref[me] = packed[me]
    all_ids_ref[sub] = ids[...]
    list_pairs(pair_ref, total_ref[0, 0], list_ref)

    def finish(step, _):
        to_home(step).wait()
        in_ref[lax.rem(me + homes - step, homes)] = got[step]
        return 0

    def finish_sub(step, _):
        to_sub(step).wait()
        all_ids_ref[lax.rem(sub + subs - step, subs)] = got_ids[step]
        return 0

    lax.fori_loop(1, homes, finish, 0, unroll=unroll)
    lax.fori_loop(1, subs, finish_sub, 0, unroll=True)


def exchange(data, kinds, info, chosen, counts, pairs, totals, subs):
    homes, capacity = chosen.shape[2:]
    width = data.shape[3]
    block = (homes, padded(FIELDS * capacity + 1), width)
    id_block = (8, homes * padded(3 * capacity))
    return pl.pallas_call(
        exchange_kernel,
        out_shape=(
            jax.ShapeDtypeStruct(block, jnp.float32),
            jax.ShapeDtypeStruct((subs,) + id_block, jnp.float32),
            jax.ShapeDtypeStruct((3, pairs.shape[2]), jnp.int32),
        ),
        in_specs=[spec(VMEM), spec(VMEM), spec(SMEM), spec(SMEM), spec(SMEM), spec(VMEM), spec(SMEM)],
        out_specs=(spec(VMEM),) * 3,
        scratch_shapes=[
            VMEM(block, jnp.float32),
            VMEM(id_block, jnp.float32),
            VMEM(block, jnp.float32),
            VMEM((subs,) + id_block, jnp.float32),
            pltpu.SemaphoreType.DMA((homes,)),
            pltpu.SemaphoreType.DMA((homes,)),
            pltpu.SemaphoreType.DMA((subs,)),
            pltpu.SemaphoreType.DMA((subs,)),
        ],
        compiler_params=pltpu.CompilerParams(collective_id=0, has_side_effects=True),
    )(
        data,
        kinds,
        jnp.transpose(info, (0, 2, 1)),
        jnp.transpose(chosen, (0, 3, 1, 2)),
        counts,
        jnp.transpose(pairs, (0, 1, 3, 2)),
        totals,
    )


def force_kernel(list_ref, rep_ref, dis_ref, in_ref, out_ref, kind_ref, rec_ref, far_ref, back_ref, slot_ref):
    slots, width = kind_ref.shape
    homes = out_ref.shape[0]
    capacity = slots // homes
    reach_sq = CUTOFF_SQ + SOFTENING
    reach = reach_sq**0.5
    scale = reach_sq * reach / (CUTOFF_SQ * CUTOFF_SQ)
    diag = lax.broadcasted_iota(jnp.int32, (width, width), 0) == lax.broadcasted_iota(jnp.int32, (width, width), 1)
    lane = lax.broadcasted_iota(jnp.int32, (1, width), 1)
    atom_row = lane.astype(jnp.float32) + 0.5

    def unpack(home, _):
        runs = in_ref[home, FIELDS * capacity : FIELDS * capacity + 1]
        for column in range(capacity):
            slot = home * capacity + column
            base = FIELDS * column
            rec_ref[slot, 0:3] = in_ref[home, base : base + 3] * (1.0 / reach)
            rec_ref[slot, 3:4] = in_ref[home, base + 3 : base + 4]
            kind_ref[pl.ds(slot, 1)] = in_ref[home, base + 4 : base + 5]
            run = jnp.sum(jnp.where(lane == column, runs, 0.0), axis=1, keepdims=True)
            rec_ref[slot, 6:7] = jnp.broadcast_to(1.0 / run, (1, width))
            slot_ref[slot] = jnp.zeros(slot_ref.shape[1:], jnp.float32)
        return 0

    lax.fori_loop(0, homes, unpack, 0, unroll=homes <= 8)
    slot_ref[slots] = jnp.zeros(slot_ref.shape[1:], jnp.float32)
    kinds = kind_ref[...]
    repulsion = jnp.zeros(kinds.shape, jnp.float32)
    dispersion = jnp.zeros(kinds.shape, jnp.float32)
    for kind in range(rep_ref.shape[0]):
        match = kinds == float(kind)
        repulsion = jnp.where(match, rep_ref[kind], repulsion)
        dispersion = jnp.where(match, dis_ref[kind], dispersion)
    rec_ref[:, 4] = repulsion
    rec_ref[:, 5] = dispersion
    back_ref[...] = jnp.zeros(back_ref.shape, jnp.float32)

    def close_group(far):
        for axis in range(3):
            folded = jnp.sum(jnp.transpose(back_ref[axis]).reshape(width // 8, 8, width), axis=0)
            slot_ref[far, axis] = slot_ref[far, axis] - folded

    def change_group(closed, far):
        rows = rec_ref[far]
        for field in range(6):
            far_ref[field] = jnp.transpose(jnp.broadcast_to(rows[field : field + 1], (width, width)))
        close_group(closed)
        back_ref[...] = jnp.zeros(back_ref.shape, jnp.float32)

    def tile_pair(near, near_scale, far_scale, own, both):
        rows = rec_ref[near]
        x, y, z = rows[0:1], rows[1:2], rows[2:3]
        charge = rows[3:4] * (far_scale * (COULOMB * scale / reach))
        rep = rows[4:5] * (far_scale * (12.0 * scale / reach_sq**6))
        dis = rows[5:6] * (far_scale * (6.0 * scale / reach_sq**3))
        if own:
            per_run = rows[6:7]
            mol = jnp.floor(atom_row * per_run)
        sums = [jnp.zeros((8, width), jnp.float32) for _ in range(3)]
        for start in range(0, width, CHUNK):
            at = slice(start, start + CHUNK)
            dx = x - far_ref[0, at]
            dy = y - far_ref[1, at]
            dz = z - far_ref[2, at]
            soft = dx * dx + dy * dy + (dz * dz + SOFTENING / reach_sq)
            root = lax.rsqrt(soft)
            inverse = root * root
            cube = inverse * inverse * inverse
            window = jnp.maximum(1.0 - soft, 0.0)
            first = (rep * far_ref[4, at]) * cube * (inverse - 2.0 / 3.0)
            second = (dis * far_ref[5, at]) * (inverse - 1.0 / 3.0)
            third = (charge * far_ref[3, at]) * root * (inverse + 3.0)
            weight = ((first - second) * cube + third) * window
            if own:
                atoms = lax.broadcasted_iota(jnp.int32, (CHUNK, width), 0).astype(jnp.float32) + (start + 0.5)
                weight = jnp.where(mol == jnp.floor(atoms * per_run), 0.0, weight)
            for axis, step in enumerate((dx, dy, dz)):
                term = weight * step
                sums[axis] = sums[axis] + jnp.sum(term.reshape(CHUNK // 8, 8, width), axis=0)
                if both:
                    back_ref[axis, at] = back_ref[axis, at] + term
        for axis in range(3):
            slot_ref[near, axis] = slot_ref[near, axis] + sums[axis] * near_scale

    used = list_ref[2, 0]

    def visit(index, open_slot):
        code = list_ref[0, index]
        tally = list_ref[1, index]
        far = code >> FAR_SHIFT
        near = code & ((1 << FAR_SHIFT) - 1)
        forward = (tally >> 8).astype(jnp.float32)
        backward_count = tally & 255
        backward = backward_count.astype(jnp.float32)

        @pl.when(far != open_slot)
        def _():
            change_group(open_slot, far)

        both = backward_count > 0

        @pl.when(both)
        def _():
            ratio = jnp.full((8, width), forward, jnp.float32) / jnp.full((8, width), backward, jnp.float32)
            tile_pair(near, ratio, backward, False, True)

        @pl.when(jnp.logical_not(both))
        def _():
            @pl.when(near == far)
            def _():
                tile_pair(near, forward, 1.0, True, False)

            @pl.when(near != far)
            def _():
                tile_pair(near, forward, 1.0, False, False)

        return far

    close_group(lax.fori_loop(0, used, visit, jnp.int32(slots)))

    def finish(home, _):
        for column in range(capacity):
            for axis in range(3):
                row = 3 * column + axis
                out_ref[home, row : row + 1] = jnp.sum(slot_ref[home * capacity + column, axis], axis=0, keepdims=True)
        for row in range(3 * capacity, out_ref.shape[1]):
            out_ref[home, row : row + 1] = jnp.zeros((1, width), jnp.float32)
        return 0

    lax.fori_loop(0, homes, finish, 0, unroll=homes <= 8)


def slot_forces(listed, repulsion, dispersion, incoming, capacity):
    homes, _, width = incoming.shape
    slots = homes * capacity
    return pl.pallas_call(
        force_kernel,
        out_shape=jax.ShapeDtypeStruct((homes, padded(3 * capacity), width), jnp.float32),
        in_specs=[spec(SMEM), spec(SMEM), spec(SMEM), spec(VMEM)],
        out_specs=spec(VMEM),
        scratch_shapes=[
            VMEM((slots, width), jnp.float32),
            VMEM((slots, 8, width), jnp.float32),
            VMEM((6, width, width), jnp.float32),
            VMEM((3, width, width), jnp.float32),
            VMEM((slots + 1, 3, 8, width), jnp.float32),
        ],
    )(listed, repulsion, dispersion, incoming)


def return_kernel(used, force_ref, ids_ref, out_ref, got, send_sem, recv_sem):
    homes, rows, width = force_ref.shape
    subs = ids_ref.shape[0]
    reps = lax.axis_size("rep")
    me = lax.axis_index("box") * reps + lax.axis_index("rep")
    sub = lax.axis_index("sub")
    total = subs * homes
    mine = sub * homes + me
    got[...] = jnp.zeros(got.shape, jnp.float32)
    barrier = pltpu.get_barrier_semaphore()

    def place(step):
        peer = lax.rem(mine + step, total)
        home = lax.rem(peer, homes)
        return home, {"sub": peer // homes, "box": home // reps, "rep": lax.rem(home, reps)}

    def greet(step, _):
        pl.semaphore_signal(barrier, inc=1, device_id=place(step)[1], device_id_type=MESH)
        return 0

    lax.fori_loop(1, total, greet, 0, unroll=total <= 16)
    pl.semaphore_wait(barrier, total - 1)

    def copy(step):
        home, device = place(step)
        return pltpu.make_async_remote_copy(
            src_ref=force_ref.at[home, pl.ds(0, used)],
            dst_ref=got.at[mine, pl.ds(0, used)],
            send_sem=send_sem.at[step],
            recv_sem=recv_sem.at[step],
            device_id=device,
            device_id_type=MESH,
        )

    def start(step, _):
        copy(1 + lax.rem(step + homes // 2 - 2, total - 1)).start()
        return 0

    def finish(step, _):
        copy(step).wait()
        return 0

    lax.fori_loop(1, total, start, 0, unroll=total <= 16)
    got[mine] = force_ref[me]
    lax.fori_loop(1, total, finish, 0, unroll=total <= 16)
    tiles = out_ref.shape[0]
    held = 3 * tiles
    wanted = lax.broadcasted_iota(jnp.int32, (held, homes * rows), 0) + sub * held
    wanted = wanted.astype(jnp.float32)
    result = jnp.zeros((held, width), jnp.float32)
    for plane in range(subs):
        pick = (ids_ref[plane, 0:1] == wanted).astype(jnp.float32)
        block = got[plane * homes : (plane + 1) * homes].reshape(homes * rows, width)
        result = result + jnp.dot(
            pick, block, precision=lax.Precision.HIGHEST, preferred_element_type=jnp.float32
        )
    for row in range(held):
        out_ref[row // 3, row % 3] = result[row : row + 1]


def send_back(forces, ids, held, used):
    homes, rows, width = forces.shape
    subs = ids.shape[0]
    return pl.pallas_call(
        functools.partial(return_kernel, used),
        out_shape=jax.ShapeDtypeStruct((held, 3, 1, width), jnp.float32),
        in_specs=[spec(VMEM), spec(VMEM)],
        out_specs=spec(VMEM),
        scratch_shapes=[
            VMEM((subs * homes, rows, width), jnp.float32),
            pltpu.SemaphoreType.DMA((subs * homes,)),
            pltpu.SemaphoreType.DMA((subs * homes,)),
        ],
        compiler_params=pltpu.CompilerParams(collective_id=1, has_side_effects=True),
    )(forces, ids)


def per_device(
    atom_data, atom_type, tile_info, lj_repulsion, lj_dispersion, send_tiles, send_count, pair_slots, pair_count
):
    subs = lax.axis_size("sub")
    incoming, ids, listed = exchange(
        atom_data, atom_type, tile_info, send_tiles, send_count, pair_slots, pair_count, subs
    )
    forces = slot_forces(listed, lj_repulsion, lj_dispersion, incoming, send_tiles.shape[3])
    result = send_back(forces, ids, atom_data.shape[1] // subs, 3 * send_tiles.shape[3])
    return jnp.transpose(result, (2, 0, 1, 3))


def solution(mesh):
    placed = (
        P(("groups", "box", "rep"), None, None, None),
        P(("groups", "box", "rep"), None, None),
        P(("groups", "box", "rep"), None, None),
        P(),
        P(),
        P(("groups", "box", "rep"), "sub", None, None),
        P(("groups", "box", "rep"), "sub", None),
        P(("groups", "box", "rep"), "sub", None, None),
        P(("groups", "box", "rep"), "sub"),
    )
    return jax.shard_map(
        per_device,
        mesh=mesh,
        in_specs=placed,
        out_specs=P(("groups", "box", "rep"), "sub", None, None),
        check_vma=False,
    )
```
